256 devices in a mesh: fac: 32 (over y, z), scn: 8 (over x, core).
Axes of the slice: x: 4, y: 4, z: 8, core: 2. Of those that a mesh axis runs over, the one named last changes fastest.
Arguments:
- loadings: bfloat16 [196608, 512], P('fac'), may hold values from -0.25 to 0.25
- draws: bfloat16 [512, 6144], P(None, 'scn'), may hold values from -6 to 6
- delta: float32 [196608], P('fac'), may hold values from -0.013671875 to 0.013671875
- gamma: bfloat16 [512, 128, 128], P('fac', 'scn'), may hold values from -0.0014648438 to 0.0014648438
- pair_rows: int32 [512], replicated, may hold values from 0 to 1535, as said below
- pair_cols: int32 [512], replicated, may hold values from 0 to 1535, as said below
- pair_count: int32 [32], replicated, may hold values from 4 to 16, as said below
Outputs:
- pnl: float32 [6144], P('scn')
The draws below stay inside these ranges and needn't reach their ends.
Inputs may be any that keep to these rules, and one draw needn't show every extreme that they name: Block numbers of the slots; for every owner o, among the 32 entries pair_rows and pair_cols of its slots (live or not), the blocks of each index h of fac (blocks h * 48 to h * 48 + 47) are named at most 2 times, and for every owner some index h is named exactly 2 times. `pair_cols`: see pair_rows; the bound holds with both lists together. An owner's live slots are its first pair_count slots; some owner has all 16 slots live.
All inputs are finite; a program needn't handle non-finite values.
Results may differ from the reference program's by a relative error of at most 0.002.
Values may be sent and summed in bfloat16 or wider, within the bound.
No kernel may reach another device: no remote copies, remote signals or barrier semaphores. Data moves between devices by JAX's collectives and lax.ppermute only.
A program may use at most 128 MiB of HBM per device.

```python
import jax
import jax.numpy as jnp
from jax import lax

BLK = 128
BLK_DEV = 48
K = 512
S_DEV = 768
CAP = 16
FACTORS = 196608
BLOCKS = 1536
PAIRS = 512
MOST = 2
SCEN = 6144
N_SCN = 8


def owner_table(owner_key):
    holders = BLOCKS // BLK_DEV
    entries = 2 * CAP
    base = MOST - 1
    index = jnp.arange(entries, dtype=jnp.int32)
    chosen = jax.random.permutation(jax.random.fold_in(owner_key, 1), holders).astype(jnp.int32)
    heavy = chosen[0]
    doubled = chosen[1]
    first_donor = chosen[2]
    second_donor = chosen[3]
    listing = index // base
    listing = jnp.where(index == first_donor * base, heavy, listing).astype(jnp.int32)
    listing = jnp.where(index == second_donor * base, doubled, listing).astype(jnp.int32)
    pulled = (index == doubled * base) | (index == second_donor * base)
    order = jnp.argsort(jnp.where(pulled, 0, 1).astype(jnp.int32), stable=True)
    remaining = listing[order][2:]
    remaining = jax.random.permutation(jax.random.fold_in(owner_key, 3), remaining)
    diag_slot = jax.random.randint(jax.random.fold_in(owner_key, 4), (), 0, CAP // 4).astype(jnp.int32)
    slot_of = index // 2
    shifted = jnp.where(index > 2 * diag_slot + 1, index - 2, index)
    shifted = jnp.clip(shifted, 0, entries - 3)
    holder = jnp.where(slot_of == diag_slot, doubled, remaining[shifted]).astype(jnp.int32)
    same_holder = holder[:, None] == holder[None, :]
    earlier = index[None, :] < index[:, None]
    within_rank = jnp.sum((same_holder & earlier).astype(jnp.int32), axis=1).astype(jnp.int32)
    holder_start = jax.random.randint(jax.random.fold_in(owner_key, 5), (holders,), 0, BLK_DEV).astype(jnp.int32)
    offset = ((holder_start[holder] + within_rank) % BLK_DEV).astype(jnp.int32)
    paired_offset = offset.reshape(CAP, 2)
    col_offset = jnp.where(jnp.arange(CAP, dtype=jnp.int32) == diag_slot, paired_offset[:, 0], paired_offset[:, 1])
    offset = jnp.stack([paired_offset[:, 0], col_offset], axis=1).reshape(-1)
    return (holder * BLK_DEV + offset).astype(jnp.int32)


def request_table(key):
    owners = PAIRS // CAP
    base = jax.random.fold_in(key, 11)
    owner_keys = jax.random.split(jax.random.fold_in(base, 1), owners)
    return jax.vmap(owner_table)(owner_keys)


def draw_pair_rows(key, part):
    return request_table(key)[:, 0::2].reshape(-1)


def draw_pair_cols(key, part):
    return request_table(key)[:, 1::2].reshape(-1)


def draw_pair_count(key, part):
    owners = PAIRS // CAP
    counts = jax.random.randint(jax.random.fold_in(key, 21), (owners,), CAP // 4, 3 * CAP // 4 + 1)
    picked = jax.random.randint(jax.random.fold_in(key, 22), (), 0, owners)
    return jnp.where(jnp.arange(owners) == picked, CAP, counts).astype(jnp.int32)


def block_levels(key, dims, cuts, smallest, top_value):
    level, own = 1.0, jax.random.fold_in(key, 6)
    for position, shards_of in cuts:
        heights = jnp.exp(jax.random.uniform(jax.random.fold_in(own, position), (shards_of,), jnp.float32, smallest / len(cuts), top_value / len(cuts)))
        level = level * jnp.repeat(heights, dims[position] // shards_of).reshape([-1 if axis == position else 1 for axis in range(len(dims))])
    return level


def normal_values(rng, shape, deviation, most, pieces=(), kind=jnp.bfloat16):
    values = jax.random.normal(rng, shape, jnp.float32) * deviation
    if len(pieces) > 0:
        values = block_levels(rng, shape, pieces, -0.22, 0.18) * values
    return jnp.clip(values, min=-most, max=most).astype(kind)


def setup_inputs(seed: int = 0) -> dict:
    streams_of = jax.random.split(jax.random.key(seed), 8)
    return {
        "loadings": normal_values(streams_of[0], (FACTORS, K), K ** -0.5, 0.25, ((0, 32),)),
        "draws": normal_values(streams_of[1], (K, SCEN), 1.0, 6.0, ((1, 8),)),
        "delta": normal_values(streams_of[2], (FACTORS,), FACTORS ** -0.5, 0.013671875, ((0, 32),), jnp.float32),
        "gamma": normal_values(streams_of[3], (PAIRS, BLK, BLK), (BLK * BLK * PAIRS * 2) ** -0.5, 0.0014648438, ((0, 32), (1, 8))),
        "pair_rows": draw_pair_rows(jax.random.fold_in(streams_of[7], 71), 0),
        "pair_cols": draw_pair_cols(jax.random.fold_in(streams_of[7], 71), 0),
        "pair_count": draw_pair_count(jax.random.fold_in(streams_of[7], 71), 0),
    }


def reference(loadings, draws, delta, gamma, pair_rows, pair_cols, pair_count):
    owners = PAIRS // CAP
    blocks = loadings.shape[0] // BLK
    is_live = jnp.arange(CAP, dtype=jnp.int32)[None, :] < pair_count[:, None]
    weight = jnp.where(pair_rows == pair_cols, 1.0, 2.0).astype(jnp.float32) * is_live.reshape(-1).astype(jnp.float32)
    gamma_owned = gamma.reshape(owners, CAP, BLK, BLK)
    rows_owned = pair_rows.reshape(owners, CAP)
    cols_owned = pair_cols.reshape(owners, CAP)
    weight_owned = weight.reshape(owners, CAP)

    def one_group(draw_block):
        exposure = jnp.dot(loadings, draw_block, preferred_element_type=jnp.float32)
        linear = jnp.sum(delta[:, None] * exposure, axis=0)
        shocks = exposure.astype(jnp.bfloat16).reshape(blocks, BLK, S_DEV)

        def per_owner(items):
            gamma_block, row_ids, col_ids, slot_weight = items
            left_block = shocks[row_ids].astype(jnp.float32)
            right_block = shocks[col_ids].astype(jnp.float32)
            product = jnp.einsum("cab,cbs->cas", gamma_block.astype(jnp.float32), right_block)
            return jnp.sum(slot_weight[:, None] * jnp.sum(product * left_block, axis=1), axis=0)

        parts = lax.map(per_owner, (gamma_owned, rows_owned, cols_owned, weight_owned))
        return linear + 0.5 * jnp.sum(parts, axis=0)

    groups = draws.reshape(K, N_SCN, S_DEV).transpose(1, 0, 2)
    return lax.map(one_group, groups).reshape(-1)
```

```python
import functools

import jax
import jax.numpy as jnp
from jax import lax
from jax.experimental import pallas as pl
from jax.experimental.pallas import tpu as pltpu
from jax.sharding import PartitionSpec as P

F32 = jnp.float32
BF16 = jnp.bfloat16
VMEM = pl.BlockSpec(memory_space=pltpu.VMEM)
SMEM = pl.BlockSpec(memory_space=pltpu.SMEM)
ANY = pl.BlockSpec(memory_space=pl.ANY)
LANES = 128
OWNERS = 32
PARTS = 8
CAP = 16
BLOCKS_DEV = 48
SLICE = 16
GROUPS = 4
UPPER = [(g, h) for g in range(GROUPS) for h in range(g, GROUPS)]


def holder_of(block):
    return (block * 1366) >> 16


def pick_kernel(ids, rows_s, cols_s, rows_v, cols_v, loadings, out, arrival, keys_v, keys_s, seen, sems, key_sem):
    me = ids[0]
    part = ids[1]
    lane = lax.broadcasted_iota(jnp.int32, rows_v.shape, 1) & (CAP - 1)

    def keyed(blocks, first_slot):
        holder = holder_of(blocks)
        key = (lane + first_slot) * 64 + (blocks - holder * BLOCKS_DEV)
        mine = holder == me
        return jnp.where(mine, key, 1 << 20), jnp.where(mine, -key, 1)

    low_r, high_r = keyed(rows_v[...], 0)
    low_c, high_c = keyed(cols_v[...], CAP)
    keys = jnp.concatenate([jnp.minimum(low_r, low_c), jnp.minimum(high_r, high_c)], axis=0)
    for shift in (1, 2, 4, 8):
        keys = jnp.minimum(keys, pltpu.roll(keys, LANES - shift, 1))
    keys_v[...] = keys
    copy = pltpu.make_async_copy(keys_v, keys_s, key_sem)
    copy.start()
    for h in range(OWNERS):
        seen[h] = 0
    for t in range(2 * CAP):
        block = rows_s[me * CAP + t] if t < CAP else cols_s[me * CAP + t - CAP]
        holder = holder_of(block)
        arrival[t] = 2 * holder + seen[holder]
        seen[holder] = 1
    copy.wait()

    def fetch(slot, offset):
        start = pl.multiple_of(offset * LANES + part * SLICE, SLICE)
        return pltpu.make_async_copy(loadings.at[pl.ds(start, SLICE), :], out.at[slot], sems.at[slot])

    for o in range(OWNERS):
        row, col = o // 8, (o % 8) * CAP
        fetch(2 * o, jnp.minimum(keys_s[row, col] & 63, BLOCKS_DEV - 1)).start()
        fetch(2 * o + 1, jnp.minimum((-keys_s[4 + row, col]) & 63, BLOCKS_DEV - 1)).start()
    for slot in range(2 * OWNERS):
        fetch(slot, 0).wait()


def regroup_kernel(arrival, recv, gamma, out):
    for t in range(2 * CAP):
        block = recv[arrival[t]]
        dest = (t % CAP) // 2
        first = ((t % 2) + 2 * (t // CAP)) * GROUPS
        for g in range(GROUPS):
            out[dest, first + g] = block[:, g * LANES : (g + 1) * LANES]
    for p in range(CAP):
        out[p // 2, 4 * GROUPS + p % 2] = gamma[p]


def pair_kernel(ids, rows_s, cols_s, count_s, recv, out):
    me = ids[0]
    part = ids[1]

    def block(b):
        tiles = [recv[:, b * GROUPS + g].reshape(LANES, LANES) for g in range(GROUPS)]
        return jnp.concatenate(tiles, axis=1)

    left = []
    high = []
    low = []
    for q in range(2):
        slot = 2 * part + q
        p = me * CAP + slot
        weight = jnp.where(rows_s[p] == cols_s[p], 0.5, 1.0)
        weight = jnp.where(slot < count_s[me], weight, 0.0)
        stored = recv[:, 4 * GROUPS + q].reshape(LANES, LANES)
        half = jnp.dot(stored, block(2 + q), preferred_element_type=F32) * weight
        top = half.astype(BF16)
        left.append(block(q))
        high.append(top)
        low.append((half - top.astype(F32)).astype(BF16))
    a = jnp.concatenate(left, axis=0)
    y = jnp.concatenate(high, axis=0)
    z = jnp.concatenate(low, axis=0)
    one = jnp.concatenate([a, a, y, z], axis=0)
    two = jnp.concatenate([y, z, a, a], axis=0)
    for k, (g, h) in enumerate(UPPER):
        summed = lax.dot_general(
            one[:, g * LANES : (g + 1) * LANES],
            two[:, h * LANES : (h + 1) * LANES],
            (((0,), (0,)), ((), ())),
            preferred_element_type=F32,
        )
        if g == h:
            summed = summed * 0.5
        out[:, k] = summed.astype(BF16).reshape(PARTS, SLICE, LANES)


def form_kernel(matrix, draws, slope, out):
    columns = draws.shape[1]
    total = jnp.zeros((1, columns), F32)
    for g in range(GROUPS):
        tiles = [
            matrix[:, k].reshape(LANES, LANES) for k, (i, _) in enumerate(UPPER) if i == g
        ]
        wide = jnp.concatenate(tiles, axis=1) if len(tiles) > 1 else tiles[0]
        image = jnp.dot(wide, draws[g * LANES :, :], preferred_element_type=F32)
        mine = draws[g * LANES : (g + 1) * LANES, :].astype(F32)
        total += jnp.sum(image * mine, axis=0, keepdims=True)
    v = slope[...]
    one = v.astype(BF16)
    v = v - one.astype(F32)
    two = v.astype(BF16)
    v = v - two.astype(F32)
    parts = jnp.concatenate(
        [one, two, v.astype(BF16), jnp.zeros((5, v.shape[1]), BF16)], axis=0
    )
    linear = jnp.dot(parts, draws[...], preferred_element_type=F32)
    total += jnp.sum(linear, axis=0, keepdims=True)
    rows = [total[:, i * LANES : (i + 1) * LANES] for i in range(columns // LANES)]
    rows += [jnp.zeros((8 - len(rows), LANES), F32)]
    tile = jnp.concatenate(rows, axis=0)
    for o in range(OWNERS):
        out[o] = tile


def on_device(loadings, draws, delta, gamma, pair_rows, pair_cols, pair_count):
    columns = draws.shape[1]
    depth = loadings.shape[1]
    ids = jnp.stack([lax.axis_index("fac"), lax.axis_index("scn")]).astype(jnp.int32)
    outgoing, arrival = pl.pallas_call(
        pick_kernel,
        out_shape=(
            jax.ShapeDtypeStruct((2 * OWNERS, SLICE, depth), BF16),
            jax.ShapeDtypeStruct((2 * CAP,), jnp.int32),
        ),
        in_specs=[SMEM, SMEM, SMEM, VMEM, VMEM, ANY],
        out_specs=(VMEM, SMEM),
        scratch_shapes=[
            pltpu.VMEM((8, LANES), jnp.int32),
            pltpu.SMEM((8, LANES), jnp.int32),
            pltpu.SMEM((OWNERS,), jnp.int32),
            pltpu.SemaphoreType.DMA((2 * OWNERS,)),
            pltpu.SemaphoreType.DMA,
        ],
        name="pick",
    )(ids, pair_rows, pair_cols, pair_rows.reshape(4, LANES), pair_cols.reshape(4, LANES), loadings)
    arrived = lax.all_to_all(outgoing, "fac", split_axis=0, concat_axis=0, tiled=True)
    slope = jnp.sum(delta[:, None] * loadings.astype(F32), axis=0)
    grouped = pl.pallas_call(
        regroup_kernel,
        out_shape=jax.ShapeDtypeStruct((PARTS, 18, SLICE, LANES), BF16),
        in_specs=[SMEM, VMEM, VMEM],
        out_specs=VMEM,
        name="regroup",
    )(arrival, arrived, gamma)
    pairs = lax.all_to_all(grouped, "scn", split_axis=0, concat_axis=0, tiled=True)
    partial = pl.pallas_call(
        pair_kernel,
        out_shape=jax.ShapeDtypeStruct((PARTS, len(UPPER), SLICE, LANES), BF16),
        in_specs=[SMEM, SMEM, SMEM, SMEM, VMEM],
        out_specs=VMEM,
        name="pair",
    )(ids, pair_rows, pair_cols, pair_count, pairs)
    partial = lax.all_to_all(partial, "scn", split_axis=0, concat_axis=0, tiled=True)
    rows = jnp.sum(partial.astype(F32), axis=0).astype(BF16)
    matrix = lax.all_gather(rows, "scn", axis=0, tiled=False)
    mine = pl.pallas_call(
        form_kernel,
        out_shape=jax.ShapeDtypeStruct((OWNERS, 8, LANES), F32),
        in_specs=[VMEM, VMEM, VMEM],
        out_specs=VMEM,
        name="form",
    )(matrix, draws, slope.reshape(1, depth))
    every = lax.all_to_all(mine, "fac", split_axis=0, concat_axis=0, tiled=True)
    return jnp.sum(every, axis=0).reshape(-1)[:columns]


def solution(mesh):
    in_specs = (P("fac", None), P(None, "scn"), P("fac"), P("fac", "scn", None), P(), P(), P())
    out_specs = P("scn")
    return jax.shard_map(
        on_device, mesh=mesh, in_specs=in_specs, out_specs=out_specs, check_vma=False
    )
```

```python
import jax
import jax.numpy as jnp
from jax import lax
from jax.experimental import pallas as pl
from jax.experimental.pallas import tpu as pltpu
from jax.sharding import PartitionSpec as P


F32 = jnp.float32
BF16 = jnp.bfloat16
VMEM = pl.BlockSpec(memory_space=pltpu.VMEM)
SMEM = pl.BlockSpec(memory_space=pltpu.SMEM)
ANY = pl.BlockSpec(memory_space=pl.ANY)
LANES = 128
OWNERS = 32
PARTS = 8
CAP = 16
BLOCKS_DEV = 48
SLICE = 16
GROUPS = 4
UPPER = [(g, h) for g in range(GROUPS) for h in range(g, GROUPS)]


def holder_of(block):
    return (block * 1366) >> 16


def pick_kernel(ids, rows_s, cols_s, rows_v, cols_v, loadings, out, arrival, keys_v, keys_s, seen, sems, key_sem):
    me = ids[0]
    part = ids[1]
    lane = lax.broadcasted_iota(jnp.int32, rows_v.shape, 1) & (CAP - 1)

    def keyed(blocks, first_slot):
        holder = holder_of(blocks)
        key = (lane + first_slot) * 64 + (blocks - holder * BLOCKS_DEV)
        mine = holder == me
        return jnp.where(mine, key, 1 << 20), jnp.where(mine, -key, 1)

    low_r, high_r = keyed(rows_v[...], 0)
    low_c, high_c = keyed(cols_v[...], CAP)
    keys = jnp.concatenate([jnp.minimum(low_r, low_c), jnp.minimum(high_r, high_c)], axis=0)
    for shift in (1, 2, 4, 8):
        keys = jnp.minimum(keys, pltpu.roll(keys, LANES - shift, 1))
    keys_v[...] = keys
    copy = pltpu.make_async_copy(keys_v, keys_s, key_sem)
    copy.start()
    for h in range(OWNERS):
        seen[h] = 0
    for t in range(2 * CAP):
        block = rows_s[me * CAP + t] if t < CAP else cols_s[me * CAP + t - CAP]
        holder = holder_of(block)
        arrival[t] = 2 * holder + seen[holder]
        seen[holder] = 1
    copy.wait()

    def fetch(slot, offset):
        start = pl.multiple_of(offset * LANES + part * SLICE, SLICE)
        return pltpu.make_async_copy(loadings.at[pl.ds(start, SLICE), :], out.at[slot], sems.at[slot])

    for o in range(OWNERS):
        row, col = o // 8, (o % 8) * CAP
        fetch(2 * o, jnp.minimum(keys_s[row, col] & 63, BLOCKS_DEV - 1)).start()
        fetch(2 * o + 1, jnp.minimum((-keys_s[4 + row, col]) & 63, BLOCKS_DEV - 1)).start()
    for slot in range(2 * OWNERS):
        fetch(slot, 0).wait()


def regroup_kernel(arrival, recv, gamma, out):
    for t in range(2 * CAP):
        block = recv[arrival[t]]
        dest = (t % CAP) // 2
        first = ((t % 2) + 2 * (t // CAP)) * GROUPS
        for g in range(GROUPS):
            out[dest, first + g] = block[:, g * LANES : (g + 1) * LANES]
    for p in range(CAP):
        out[p // 2, 4 * GROUPS + p % 2] = gamma[p]


def pair_kernel(ids, rows_s, cols_s, count_s, recv, out):
    me = ids[0]
    part = ids[1]

    def block(b):
        tiles = [recv[:, b * GROUPS + g].reshape(LANES, LANES) for g in range(GROUPS)]
        return jnp.concatenate(tiles, axis=1)

    left = []
    high = []
    low = []
    for q in range(2):
        slot = 2 * part + q
        p = me * CAP + slot
        weight = jnp.where(rows_s[p] == cols_s[p], 0.5, 1.0)
        weight = jnp.where(slot < count_s[me], weight, 0.0)
        stored = recv[:, 4 * GROUPS + q].reshape(LANES, LANES)
        half = jnp.dot(stored, block(2 + q), preferred_element_type=F32) * weight
        top = half.astype(BF16)
        left.append(block(q))
        high.append(top)
        low.append((half - top.astype(F32)).astype(BF16))
    a = jnp.concatenate(left, axis=0)
    y = jnp.concatenate(high, axis=0)
    z = jnp.concatenate(low, axis=0)
    one = jnp.concatenate([a, a, y, z], axis=0)
    two = jnp.concatenate([y, z, a, a], axis=0)
    for k, (g, h) in enumerate(UPPER):
        summed = lax.dot_general(
            one[:, g * LANES : (g + 1) * LANES],
            two[:, h * LANES : (h + 1) * LANES],
            (((0,), (0,)), ((), ())),
            preferred_element_type=F32,
        )
        if g == h:
            summed = summed * 0.5
        out[k] = summed


def form_kernel(ids, own, other, here, left, right, far, slope, out):
    columns = here.shape[1]
    chip = ids[1] // 2
    blocks = [(own[k] + other[k]).astype(BF16) for k in range(len(UPPER))]
    wide = [
        jnp.concatenate([b for b, (i, _) in zip(blocks, UPPER) if i == g], axis=1)
        for g in range(GROUPS)
    ]

    def store(position, total):
        rows = [total[:, i * LANES : (i + 1) * LANES] for i in range(columns // LANES)]
        rows += [jnp.zeros((8 - len(rows), LANES), F32)]
        out[position] = jnp.concatenate(rows, axis=0)

    def quadratic(rows_of):
        total = jnp.zeros((1, columns), F32)
        for g in range(GROUPS):
            image = jnp.dot(wide[g], rows_of(g * LANES, None), preferred_element_type=F32)
            mine = rows_of(g * LANES, (g + 1) * LANES).astype(F32)
            total += jnp.sum(image * mine, axis=0, keepdims=True)
        return total

    v = slope[...]
    one = v.astype(BF16)
    v = v - one.astype(F32)
    two = v.astype(BF16)
    v = v - two.astype(F32)
    parts = jnp.concatenate(
        [one, two, v.astype(BF16), jnp.zeros((5, v.shape[1]), BF16)], axis=0
    )
    linear = jnp.dot(parts, here[...], preferred_element_type=F32)
    linear = jnp.sum(linear, axis=0, keepdims=True)
    store(chip, quadratic(lambda a, b: here[a:b, :]) + linear)
    store((chip + 3) & 3, quadratic(lambda a, b: left[a:b, :]))
    store((chip + 1) & 3, quadratic(lambda a, b: right[a:b, :]))
    store((chip + 2) & 3, quadratic(lambda a, b: far[a:b, :]))


def ring(step):
    return [(i, (i + step) % PARTS) for i in range(PARTS)]


def body(loadings, draws, delta, gamma, pair_rows, pair_cols, pair_count):
    columns = draws.shape[1]
    depth = loadings.shape[1]
    ids = jnp.stack([lax.axis_index("fac"), lax.axis_index("scn")]).astype(jnp.int32)
    left = lax.ppermute(draws, "scn", ring(2))
    right = lax.ppermute(draws, "scn", ring(-2))
    far = lax.ppermute(draws, "scn", ring(4))
    outgoing, arrival = pl.pallas_call(
        pick_kernel,
        out_shape=(
            jax.ShapeDtypeStruct((2 * OWNERS, SLICE, depth), BF16),
            jax.ShapeDtypeStruct((2 * CAP,), jnp.int32),
        ),
        in_specs=[SMEM, SMEM, SMEM, VMEM, VMEM, ANY],
        out_specs=(VMEM, SMEM),
        scratch_shapes=[
            pltpu.VMEM((8, LANES), jnp.int32),
            pltpu.SMEM((8, LANES), jnp.int32),
            pltpu.SMEM((OWNERS,), jnp.int32),
            pltpu.SemaphoreType.DMA((2 * OWNERS,)),
            pltpu.SemaphoreType.DMA,
        ],
        name="pick",
    )(ids, pair_rows, pair_cols, pair_rows.reshape(4, LANES), pair_cols.reshape(4, LANES), loadings)
    arrived = lax.all_to_all(outgoing, "fac", split_axis=0, concat_axis=0, tiled=True)
    slope = jnp.sum(delta[:, None] * loadings.astype(F32), axis=0)
    grouped = pl.pallas_call(
        regroup_kernel,
        out_shape=jax.ShapeDtypeStruct((PARTS, 18, SLICE, LANES), BF16),
        in_specs=[SMEM, VMEM, VMEM],
        out_specs=VMEM,
        name="regroup",
    )(arrival, arrived, gamma)
    pairs = lax.all_to_all(grouped, "scn", split_axis=0, concat_axis=0, tiled=True)
    own = pl.pallas_call(
        pair_kernel,
        out_shape=jax.ShapeDtypeStruct((len(UPPER), LANES, LANES), F32),
        in_specs=[SMEM, SMEM, SMEM, SMEM, VMEM],
        out_specs=VMEM,
        name="pair",
    )(ids, pair_rows, pair_cols, pair_count, pairs)
    other = lax.ppermute(own, "scn", [(i, i ^ 1) for i in range(PARTS)])
    spread = pl.pallas_call(
        form_kernel,
        out_shape=jax.ShapeDtypeStruct((PARTS // 2, 8, LANES), F32),
        in_specs=[SMEM] + [VMEM] * 7,
        out_specs=VMEM,
        name="form",
    )(ids, own, other, draws, left, right, far, slope.reshape(1, depth))
    chips = [[c + 2 * x for x in range(PARTS // 2)] for c in range(2)]
    along = lax.all_to_all(
        spread, "scn", split_axis=0, concat_axis=0, tiled=True, axis_index_groups=chips
    )
    mine = jnp.broadcast_to(jnp.sum(along, axis=0)[None], (OWNERS, 8, LANES))
    every = lax.all_to_all(mine, "fac", split_axis=0, concat_axis=0, tiled=True)
    return jnp.sum(every, axis=0).reshape(-1)[:columns]


def solution(mesh):
    in_specs = (P("fac", None), P(None, "scn"), P("fac"), P("fac", "scn", None), P(), P(), P())
    out_specs = P("scn")
    return jax.shard_map(body, mesh=mesh, in_specs=in_specs, out_specs=out_specs, check_vma=False)
```

```python
import jax
import jax.numpy as jnp
from jax import lax
from jax.experimental import pallas as pl
from jax.experimental.pallas import tpu as pltpu
from jax.sharding import PartitionSpec as P


F32 = jnp.float32
BF16 = jnp.bfloat16
VMEM = pl.BlockSpec(memory_space=pltpu.VMEM)
SMEM = pl.BlockSpec(memory_space=pltpu.SMEM)
HBM = pl.BlockSpec(memory_space=pltpu.HBM)
GRANT = pltpu.CompilerParams(vmem_limit_bytes=24 * 1024 * 1024)
LANES = 128
OWNERS = 32
PARTS = 8
CAP = 16
BLOCKS_DEV = 48
SLICE = 16
GROUPS = 4
UPPER = [(g, h) for g in range(GROUPS) for h in range(g, GROUPS)]


def near(x):
    return pltpu.with_memory_space_constraint(x, pltpu.VMEM)


def away(x):
    return pltpu.with_memory_space_constraint(x, pltpu.HBM)


def holder_of(block):
    return (block * 1366) >> 16


def pick_kernel(rows_s, cols_s, rows_v, cols_v, loadings, out, arrival, keys_v, keys_s, seen, sems, key_sem):
    me = lax.axis_index("fac")
    part = lax.axis_index("scn")
    lane = lax.broadcasted_iota(jnp.int32, rows_v.shape, 1) & (CAP - 1)

    def keyed(blocks, first_slot):
        holder = holder_of(blocks)
        key = (lane + first_slot) * 64 + (blocks - holder * BLOCKS_DEV)
        mine = holder == me
        return jnp.where(mine, key, 1 << 20), jnp.where(mine, -key, 1)

    low_r, high_r = keyed(rows_v[...], 0)
    low_c, high_c = keyed(cols_v[...], CAP)
    keys = jnp.concatenate([jnp.minimum(low_r, low_c), jnp.minimum(high_r, high_c)], axis=0)
    for shift in (1, 2, 4, 8):
        keys = jnp.minimum(keys, pltpu.roll(keys, LANES - shift, 1))
    keys_v[...] = keys
    copy = pltpu.make_async_copy(keys_v, keys_s, key_sem)
    copy.start()
    copy.wait()

    def fetch(slot, offset):
        start = pl.multiple_of(offset * LANES + part * SLICE, SLICE)
        return pltpu.make_async_copy(loadings.at[pl.ds(start, SLICE), :], out.at[slot], sems.at[slot])

    for o in range(OWNERS):
        row, col = o // 8, (o % 8) * CAP
        fetch(2 * o, jnp.minimum(keys_s[row, col] & 63, BLOCKS_DEV - 1)).start()
        fetch(2 * o + 1, jnp.minimum((-keys_s[4 + row, col]) & 63, BLOCKS_DEV - 1)).start()
    for h in range(OWNERS):
        seen[h] = 0
    for t in range(2 * CAP):
        block = rows_s[me * CAP + t] if t < CAP else cols_s[me * CAP + t - CAP]
        holder = holder_of(block)
        arrival[t] = 2 * holder + seen[holder]
        seen[holder] = 1
    for slot in range(2 * OWNERS):
        fetch(slot, 0).wait()


def regroup_kernel(arrival, recv, gamma, out):
    for t in range(2 * CAP):
        block = recv[arrival[t]]
        dest = (t % CAP) // 2
        first = ((t % 2) + 2 * (t // CAP)) * GROUPS
        for g in range(GROUPS):
            out[dest, first + g] = block[:, g * LANES : (g + 1) * LANES]
    for p in range(CAP):
        out[p // 2, 4 * GROUPS + p % 2] = gamma[p]


def pair_kernel(rows_s, cols_s, count_s, recv, out):
    me = lax.axis_index("fac")
    part = lax.axis_index("scn")

    def block(b):
        tiles = [recv[:, b * GROUPS + g].reshape(LANES, LANES) for g in range(GROUPS)]
        return jnp.concatenate(tiles, axis=1)

    left = []
    high = []
    low = []
    for q in range(2):
        slot = 2 * part + q
        p = me * CAP + slot
        weight = jnp.where(rows_s[p] == cols_s[p], 0.5, 1.0)
        weight = jnp.where(slot < count_s[me], weight, 0.0)
        stored = recv[:, 4 * GROUPS + q].reshape(LANES, LANES)
        half = jnp.dot(stored, block(2 + q), preferred_element_type=F32) * weight
        top = half.astype(BF16)
        left.append(block(q))
        high.append(top)
        low.append((half - top.astype(F32)).astype(BF16))
    a = jnp.concatenate(left, axis=0)
    y = jnp.concatenate(high, axis=0)
    z = jnp.concatenate(low, axis=0)
    one = jnp.concatenate([a, a, y, z], axis=0)
    two = jnp.concatenate([y, z, a, a], axis=0)
    for k, (g, h) in enumerate(UPPER):
        summed = lax.dot_general(
            one[:, g * LANES : (g + 1) * LANES],
            two[:, h * LANES : (h + 1) * LANES],
            (((0,), (0,)), ((), ())),
            preferred_element_type=F32,
        )
        if g == h:
            summed = summed * 0.5
        out[k] = summed


def form_kernel(own, other, here, left, right, far, slope, out):
    columns = here.shape[1]
    chip = lax.axis_index("scn") // 2
    blocks = [(own[k] + other[k]).astype(BF16) for k in range(len(UPPER))]
    wide = [
        jnp.concatenate([b for b, (i, _) in zip(blocks, UPPER) if i == g], axis=1)
        for g in range(GROUPS)
    ]

    def store(position, total):
        rows = [total[:, i * LANES : (i + 1) * LANES] for i in range(columns // LANES)]
        rows += [jnp.zeros((8 - len(rows), LANES), F32)]
        out[position] = jnp.concatenate(rows, axis=0)

    def quadratic(rows_of):
        total = jnp.zeros((1, columns), F32)
        for g in range(GROUPS):
            image = jnp.dot(wide[g], rows_of(g * LANES, None), preferred_element_type=F32)
            mine = rows_of(g * LANES, (g + 1) * LANES).astype(F32)
            total += jnp.sum(image * mine, axis=0, keepdims=True)
        return total

    v = slope[...]
    one = v.astype(BF16)
    v = v - one.astype(F32)
    two = v.astype(BF16)
    v = v - two.astype(F32)
    parts = jnp.concatenate(
        [one, two, v.astype(BF16), jnp.zeros((5, v.shape[1]), BF16)], axis=0
    )
    for step, rows_of in enumerate((here, right, far, left)):
        linear = jnp.dot(parts, rows_of[...], preferred_element_type=F32)
        linear = jnp.sum(linear, axis=0, keepdims=True)
        store((chip + step) & 3, quadratic(lambda a, b: rows_of[a:b, :]) + linear)


def ring(step):
    return [(i, (i + step) % PARTS) for i in range(PARTS)]


def body(loadings, draws, delta, gamma, pair_rows, pair_cols, pair_count):
    columns = draws.shape[1]
    depth = loadings.shape[1]
    rows, cols = away(pair_rows), away(pair_cols)
    left = lax.ppermute(draws, "scn", ring(2))
    right = lax.ppermute(draws, "scn", ring(-2))
    far = lax.ppermute(draws, "scn", ring(4))
    outgoing, arrival = pl.pallas_call(
        pick_kernel,
        out_shape=(
            pltpu.VMEM((2 * OWNERS, SLICE, depth), BF16),
            jax.ShapeDtypeStruct((2 * CAP,), jnp.int32),
        ),
        in_specs=[SMEM, SMEM, VMEM, VMEM, HBM],
        out_specs=(VMEM, SMEM),
        scratch_shapes=[
            pltpu.VMEM((8, LANES), jnp.int32),
            pltpu.SMEM((8, LANES), jnp.int32),
            pltpu.SMEM((OWNERS,), jnp.int32),
            pltpu.SemaphoreType.DMA((2 * OWNERS,)),
            pltpu.SemaphoreType.DMA,
        ],
        compiler_params=GRANT,
        name="pick",
    )(rows, cols, away(pair_rows.reshape(4, LANES)), away(pair_cols.reshape(4, LANES)), away(loadings))
    arrived = lax.all_to_all(outgoing, "fac", split_axis=0, concat_axis=0, tiled=True)
    chip = lax.axis_index("scn") // 2
    quarter = loadings.shape[0] // (PARTS // 2)
    some = lax.dynamic_slice_in_dim(loadings, chip * quarter, quarter)
    shares = lax.dynamic_slice_in_dim(delta, chip * quarter, quarter)
    slope = jnp.sum(shares[:, None] * some.astype(F32), axis=0)
    grouped = pl.pallas_call(
        regroup_kernel,
        out_shape=pltpu.VMEM((PARTS, 18, SLICE, LANES), BF16),
        in_specs=[SMEM, VMEM, VMEM],
        out_specs=VMEM,
        compiler_params=GRANT,
        name="regroup",
    )(arrival, near(arrived), gamma)
    pairs = lax.all_to_all(grouped, "scn", split_axis=0, concat_axis=0, tiled=True)
    own = pl.pallas_call(
        pair_kernel,
        out_shape=pltpu.VMEM((len(UPPER), LANES, LANES), F32),
        in_specs=[SMEM, SMEM, SMEM, VMEM],
        out_specs=VMEM,
        compiler_params=GRANT,
        name="pair",
    )(rows, cols, away(pair_count), near(pairs))
    other = lax.ppermute(own, "scn", [(i, i ^ 1) for i in range(PARTS)])
    spread = pl.pallas_call(
        form_kernel,
        out_shape=pltpu.VMEM((PARTS // 2, 8, LANES), F32),
        in_specs=[VMEM] * 7,
        out_specs=VMEM,
        compiler_params=GRANT,
        name="form",
    )(near(own), near(other), draws, near(left), near(right), near(far), slope.reshape(1, depth))
    chips = [[c + 2 * x for x in range(PARTS // 2)] for c in range(2)]
    along = lax.all_to_all(
        spread, "scn", split_axis=0, concat_axis=0, tiled=True, axis_index_groups=chips
    )
    mine = jnp.broadcast_to(jnp.sum(along, axis=0)[None], (OWNERS, 8, LANES))
    every = lax.all_to_all(mine, "fac", split_axis=0, concat_axis=0, tiled=True)
    return jnp.sum(every, axis=0).reshape(-1)[:columns]


def solution(mesh):
    in_specs = (P("fac", None), P(None, "scn"), P("fac"), P("fac", "scn", None), P(), P(), P())
    out_specs = P("scn")
    return jax.shard_map(body, mesh=mesh, in_specs=in_specs, out_specs=out_specs, check_vma=False)
```

```python
import jax
import jax.numpy as jnp
from jax import lax
from jax.experimental import pallas as pl
from jax.experimental.pallas import tpu as pltpu
from jax.sharding import PartitionSpec as P


F32 = jnp.float32
BF16 = jnp.bfloat16
VMEM = pl.BlockSpec(memory_space=pltpu.VMEM)
SMEM = pl.BlockSpec(memory_space=pltpu.SMEM)
HBM = pl.BlockSpec(memory_space=pltpu.HBM)
GRANT = pltpu.CompilerParams(vmem_limit_bytes=24 * 1024 * 1024)
LANES = 128
OWNERS = 32
PARTS = 8
CAP = 16
BLOCKS_DEV = 48
SLICE = 16
GROUPS = 4
WIDE = 256


def near(x):
    return pltpu.with_memory_space_constraint(x, pltpu.VMEM)


def away(x):
    return pltpu.with_memory_space_constraint(x, pltpu.HBM)


def holder_of(block):
    return (block * 1366) >> 16


def pick_kernel(
    rows, cols, count, loadings, out, table,
    rows_v, cols_v, rows_s, cols_s, count_s, keys_v, keys_s, seen, sems, small,
):
    me = lax.axis_index("fac")
    part = lax.axis_index("scn")
    pairs = ((rows, rows_v), (cols, cols_v), (rows, rows_s), (cols, cols_s), (count, count_s))
    moves = [pltpu.make_async_copy(a, b, small.at[i]) for i, (a, b) in enumerate(pairs)]
    for move in moves:
        move.start()
    moves[0].wait()
    moves[1].wait()
    lane = lax.broadcasted_iota(jnp.int32, rows_v.shape, 1) & (CAP - 1)

    def keyed(blocks, first_slot):
        holder = holder_of(blocks)
        key = (lane + first_slot) * 64 + (blocks - holder * BLOCKS_DEV)
        mine = holder == me
        return jnp.where(mine, key, 1 << 20), jnp.where(mine, -key, 1)

    low_r, high_r = keyed(rows_v[...], 0)
    low_c, high_c = keyed(cols_v[...], CAP)
    keys = jnp.concatenate([jnp.minimum(low_r, low_c), jnp.minimum(high_r, high_c)], axis=0)
    for shift in (1, 2, 4, 8):
        keys = jnp.minimum(keys, pltpu.roll(keys, LANES - shift, 1))
    keys_v[...] = keys
    copy = pltpu.make_async_copy(keys_v, keys_s, small.at[5])
    copy.start()
    copy.wait()

    def fetch(slot, offset):
        start = pl.multiple_of(offset * LANES + part * SLICE, SLICE)
        return pltpu.make_async_copy(loadings.at[pl.ds(start, SLICE), :], out.at[slot], sems.at[slot])

    for o in range(OWNERS):
        row, col = o // 8, (o % 8) * CAP
        fetch(2 * o, jnp.minimum(keys_s[row, col] & 63, BLOCKS_DEV - 1)).start()
        fetch(2 * o + 1, jnp.minimum((-keys_s[4 + row, col]) & 63, BLOCKS_DEV - 1)).start()
    for move in moves[2:]:
        move.wait()
    for h in range(OWNERS):
        seen[h] = 0
    row = me // 8
    col = (me % 8) * CAP
    for t in range(2 * CAP):
        block = rows_s[row, col + t] if t < CAP else cols_s[row, col + t - CAP]
        holder = holder_of(block)
        table[t] = 2 * holder + seen[holder]
        seen[holder] = 1
    live = count_s[me]
    for p in range(CAP):
        weight = jnp.where(rows_s[row, col + p] == cols_s[row, col + p], 1, 2)
        table[2 * CAP + p] = jnp.where(p < live, weight, 0)
    for slot in range(2 * OWNERS):
        fetch(slot, 0).wait()


def regroup_kernel(table, recv, gamma, out):
    for t in range(2 * CAP):
        block = recv[table[t]]
        dest = (t % CAP) // 2
        first = ((t % 2) + 2 * (t // CAP)) * GROUPS
        for g in range(GROUPS):
            out[dest, first + g] = block[:, g * LANES : (g + 1) * LANES]
    for p in range(CAP):
        weight = table[2 * CAP + p].astype(F32)
        out[p // 2, 4 * GROUPS + p % 2] = (gamma[p].astype(F32) * weight).astype(BF16)


def pair_kernel(recv, out):
    def block(b):
        tiles = [recv[:, b * GROUPS + g].reshape(LANES, LANES) for g in range(GROUPS)]
        return jnp.concatenate(tiles, axis=1)

    left = []
    high = []
    low = []
    for q in range(2):
        stored = recv[:, 4 * GROUPS + q].reshape(LANES, LANES)
        half = jnp.dot(stored, block(2 + q), preferred_element_type=F32)
        top = half.astype(BF16)
        left.append(block(q))
        high.append(top)
        low.append((half - top.astype(F32)).astype(BF16))
    a = jnp.concatenate(left, axis=0)
    y = jnp.concatenate(high, axis=0)
    z = jnp.concatenate(low, axis=0)
    turned = jnp.concatenate([a.T, a.T, y.T, z.T], axis=1)
    other = jnp.concatenate([y, z, a, a], axis=0)
    out[0] = 0.25 * jnp.dot(turned[:WIDE], other[:, :WIDE], preferred_element_type=F32)
    right = jnp.dot(turned, other[:, WIDE:], preferred_element_type=F32)
    out[1] = 0.5 * right[:WIDE]
    out[2] = 0.25 * right[WIDE:]


def form_kernel(own, other, here, left, right, far, slope, out):
    chip = lax.axis_index("scn") // 2
    v = slope[...]
    one = v.astype(BF16)
    v = v - one.astype(F32)
    two = v.astype(BF16)
    v = v - two.astype(F32)
    fill = jnp.zeros((13, v.shape[1]), BF16)
    parts = jnp.concatenate([one, two, v.astype(BF16), fill], axis=0)
    first = (own[0] + other[0]).astype(BF16)
    cross = (own[1] + other[1]).astype(BF16)
    last = (own[2] + other[2]).astype(BF16)
    top = jnp.concatenate([first, parts[:, :WIDE]], axis=0)
    low = jnp.concatenate([cross, parts[:, WIDE:], last], axis=0)
    extra = WIDE + parts.shape[0]
    for step, group in enumerate((here, right, far, left)):
        upper = group[:WIDE, :]
        lower = group[WIDE:, :]
        image = jnp.dot(low, lower, preferred_element_type=F32)
        more = image[:extra] + jnp.dot(top, upper, preferred_element_type=F32)
        total = jnp.sum(more[:WIDE] * upper.astype(F32) + image[extra:] * lower.astype(F32), axis=0, keepdims=True)
        out[(chip + step) & 3] = total + jnp.sum(more[WIDE:], axis=0, keepdims=True)


def ring(step):
    return [(i, (i + step) % PARTS) for i in range(PARTS)]


def body(loadings, draws, delta, gamma, pair_rows, pair_cols, pair_count):
    columns = draws.shape[1]
    depth = loadings.shape[1]
    left = lax.ppermute(draws, "scn", ring(2))
    right = lax.ppermute(draws, "scn", ring(-2))
    far = lax.ppermute(draws, "scn", ring(4))
    outgoing, table = pl.pallas_call(
        pick_kernel,
        out_shape=(
            pltpu.VMEM((2 * OWNERS, SLICE, depth), BF16),
            jax.ShapeDtypeStruct((3 * CAP,), jnp.int32),
        ),
        in_specs=[HBM, HBM, HBM, HBM],
        out_specs=(VMEM, SMEM),
        scratch_shapes=[
            pltpu.VMEM((4, LANES), jnp.int32),
            pltpu.VMEM((4, LANES), jnp.int32),
            pltpu.SMEM((4, LANES), jnp.int32),
            pltpu.SMEM((4, LANES), jnp.int32),
            pltpu.SMEM((OWNERS,), jnp.int32),
            pltpu.VMEM((8, LANES), jnp.int32),
            pltpu.SMEM((8, LANES), jnp.int32),
            pltpu.SMEM((OWNERS,), jnp.int32),
            pltpu.SemaphoreType.DMA((2 * OWNERS,)),
            pltpu.SemaphoreType.DMA((6,)),
        ],
        compiler_params=GRANT,
        name="pick",
    )(
        away(pair_rows.reshape(4, LANES)),
        away(pair_cols.reshape(4, LANES)),
        away(pair_count),
        away(loadings),
    )
    arrived = lax.all_to_all(outgoing, "fac", split_axis=0, concat_axis=0, tiled=True)
    chip = lax.axis_index("scn") // 2
    quarter = loadings.shape[0] // (PARTS // 2)
    some = lax.dynamic_slice_in_dim(loadings, chip * quarter, quarter)
    shares = lax.dynamic_slice_in_dim(delta, chip * quarter, quarter)
    slope = jnp.sum(shares[:, None] * some.astype(F32), axis=0)
    grouped = pl.pallas_call(
        regroup_kernel,
        out_shape=pltpu.VMEM((PARTS, 18, SLICE, LANES), BF16),
        in_specs=[SMEM, VMEM, VMEM],
        out_specs=VMEM,
        compiler_params=GRANT,
        name="regroup",
    )(table, near(arrived), gamma)
    pairs = lax.all_to_all(grouped, "scn", split_axis=0, concat_axis=0, tiled=True)
    own = pl.pallas_call(
        pair_kernel,
        out_shape=pltpu.VMEM((3, WIDE, WIDE), F32),
        in_specs=[VMEM],
        out_specs=VMEM,
        compiler_params=GRANT,
        name="pair",
    )(near(pairs))
    other = lax.ppermute(own, "scn", [(i, i ^ 1) for i in range(PARTS)])
    spread = pl.pallas_call(
        form_kernel,
        out_shape=pltpu.VMEM((PARTS // 2, 1, columns), F32),
        in_specs=[VMEM] * 7,
        out_specs=VMEM,
        compiler_params=GRANT,
        name="form",
    )(near(own), near(other), draws, near(left), near(right), near(far), slope.reshape(1, depth))
    chips = [[c + 2 * x for x in range(PARTS // 2)] for c in range(2)]
    along = lax.all_to_all(
        spread, "scn", split_axis=0, concat_axis=0, tiled=True, axis_index_groups=chips
    )
    mine = jnp.broadcast_to(jnp.sum(along, axis=0)[None], (OWNERS, 1, columns))
    every = lax.all_to_all(mine, "fac", split_axis=0, concat_axis=0, tiled=True)
    return jnp.sum(every, axis=0).reshape(-1)


def solution(mesh):
    in_specs = (P("fac", None), P(None, "scn"), P("fac"), P("fac", "scn", None), P(), P(), P())
    out_specs = P("scn")
    return jax.shard_map(body, mesh=mesh, in_specs=in_specs, out_specs=out_specs, check_vma=False)
```

```python
import jax
import jax.numpy as jnp
from jax import lax
from jax.experimental import pallas as pl
from jax.experimental.pallas import tpu as pltpu
from jax.sharding import PartitionSpec as P


F32 = jnp.float32
BF16 = jnp.bfloat16
VMEM = pl.BlockSpec(memory_space=pltpu.VMEM)
SMEM = pl.BlockSpec(memory_space=pltpu.SMEM)
HBM = pl.BlockSpec(memory_space=pltpu.HBM)
GRANT = pltpu.CompilerParams(vmem_limit_bytes=24 * 1024 * 1024)
LANES = 128
OWNERS = 32
PARTS = 8
CAP = 16
BLOCKS_DEV = 48
SLICE = 16
GROUPS = 4
WIDE = 256
CHIPS = 4
TILES = 18


def near(x):
    return pltpu.with_memory_space_constraint(x, pltpu.VMEM)


def away(x):
    return pltpu.with_memory_space_constraint(x, pltpu.HBM)


def holder_of(block):
    return (block * 1366) >> 16


def pick_kernel(
    rows, cols, count, loadings, out, table,
    rows_v, cols_v, rows_s, cols_s, count_s, keys_v, keys_s, seen, sems, small,
):
    me = lax.axis_index("fac")
    part = lax.axis_index("scn")
    pairs = ((rows, rows_v), (cols, cols_v), (rows, rows_s), (cols, cols_s), (count, count_s))
    moves = [pltpu.make_async_copy(a, b, small.at[i]) for i, (a, b) in enumerate(pairs)]
    for move in moves:
        move.start()
    moves[0].wait()
    moves[1].wait()
    lane = lax.broadcasted_iota(jnp.int32, rows_v.shape, 1) & (CAP - 1)

    def keyed(blocks, first_slot):
        holder = holder_of(blocks)
        key = (lane + first_slot) * 64 + (blocks - holder * BLOCKS_DEV)
        mine = holder == me
        return jnp.where(mine, key, 1 << 20), jnp.where(mine, -key, 1)

    low_r, high_r = keyed(rows_v[...], 0)
    low_c, high_c = keyed(cols_v[...], CAP)
    keys = jnp.concatenate([jnp.minimum(low_r, low_c), jnp.minimum(high_r, high_c)], axis=0)
    for shift in (1, 2, 4, 8):
        keys = jnp.minimum(keys, pltpu.roll(keys, LANES - shift, 1))
    keys_v[...] = keys
    copy = pltpu.make_async_copy(keys_v, keys_s, small.at[5])
    copy.start()
    copy.wait()

    def fetch(slot, offset):
        start = pl.multiple_of(offset * LANES + part * SLICE, SLICE)
        return pltpu.make_async_copy(loadings.at[pl.ds(start, SLICE), :], out.at[slot], sems.at[slot])

    for o in range(OWNERS):
        row, col = o // 8, (o % 8) * CAP
        fetch(2 * o, jnp.minimum(keys_s[row, col] & 63, BLOCKS_DEV - 1)).start()
        fetch(2 * o + 1, jnp.minimum((-keys_s[4 + row, col]) & 63, BLOCKS_DEV - 1)).start()
    for move in moves[2:]:
        move.wait()
    for h in range(OWNERS):
        seen[h] = 0
    row = me // 8
    col = (me % 8) * CAP
    for t in range(2 * CAP):
        block = rows_s[row, col + t] if t < CAP else cols_s[row, col + t - CAP]
        holder = holder_of(block)
        table[t] = 2 * holder + seen[holder]
        seen[holder] = 1
    live = count_s[me]
    for p in range(CAP):
        weight = jnp.where(rows_s[row, col + p] == cols_s[row, col + p], 1, 2)
        table[2 * CAP + p] = jnp.where(p < live, weight, 0)
    for slot in range(2 * OWNERS):
        fetch(slot, 0).wait()


def regroup_kernel(table, recv, gamma, keep, send):
    part = lax.axis_index("scn")
    chip = part // 2
    core = part % 2
    for step in range(CHIPS):
        for out, column in ((keep, core), (send, 1 - core)):
            first = 4 * ((chip + step) & 3) + 2 * column
            for q in range(2):
                for side in range(2):
                    block = recv[table[first + q + side * CAP]]
                    for g in range(GROUPS):
                        out[step, (q + 2 * side) * GROUPS + g] = block[:, g * LANES : (g + 1) * LANES]
                weight = table[2 * CAP + first + q].astype(F32)
                out[step, 4 * GROUPS + q] = (gamma[first + q].astype(F32) * weight).astype(BF16)


def merge_kernel(keep, swapped, *outs):
    core = lax.axis_index("scn") % 2
    for step, out in enumerate(outs):
        out[core] = keep[step]
        out[1 - core] = swapped[step]


def pair_kernel(here, one_off, two_off, three_off, out, recv):
    chip = lax.axis_index("scn") // 2
    for step, chunk in enumerate((here, one_off, two_off, three_off)):
        source = (chip + CHIPS - step) & 3
        for core in range(2):
            recv[:, 2 * source + core] = chunk[core]

    def block(b):
        tiles = [recv[b * GROUPS + g].reshape(LANES, LANES) for g in range(GROUPS)]
        return jnp.concatenate(tiles, axis=1)

    left = []
    high = []
    low = []
    for q in range(2):
        stored = recv[4 * GROUPS + q].reshape(LANES, LANES)
        half = jnp.dot(stored, block(2 + q), preferred_element_type=F32)
        top = half.astype(BF16)
        left.append(block(q))
        high.append(top)
        low.append((half - top.astype(F32)).astype(BF16))
    a = jnp.concatenate(left, axis=0)
    y = jnp.concatenate(high, axis=0)
    z = jnp.concatenate(low, axis=0)
    turned = jnp.concatenate([a.T, a.T, y.T, z.T], axis=1)
    other = jnp.concatenate([y, z, a, a], axis=0)
    out[0] = 0.25 * jnp.dot(turned[:WIDE], other[:, :WIDE], preferred_element_type=F32)
    right = jnp.dot(turned, other[:, WIDE:], preferred_element_type=F32)
    out[1] = 0.5 * right[:WIDE]
    out[2] = 0.25 * right[WIDE:]


def form_kernel(own, other, here, left, right, far, slope, *outs):
    v = slope[...]
    one = v.astype(BF16)
    v = v - one.astype(F32)
    two = v.astype(BF16)
    v = v - two.astype(F32)
    fill = jnp.zeros((13, v.shape[1]), BF16)
    parts = jnp.concatenate([one, two, v.astype(BF16), fill], axis=0)
    first = (own[0] + other[0]).astype(BF16)
    cross = (own[1] + other[1]).astype(BF16)
    last = (own[2] + other[2]).astype(BF16)
    top = jnp.concatenate([first, parts[:, :WIDE]], axis=0)
    low = jnp.concatenate([cross, parts[:, WIDE:], last], axis=0)
    extra = WIDE + parts.shape[0]
    for group, out in zip((here, right, far, left), outs):
        upper = group[:WIDE, :]
        lower = group[WIDE:, :]
        image = jnp.dot(low, lower, preferred_element_type=F32)
        more = image[:extra] + jnp.dot(top, upper, preferred_element_type=F32)
        total = jnp.sum(more[:WIDE] * upper.astype(F32) + image[extra:] * lower.astype(F32), axis=0, keepdims=True)
        out[...] = total + jnp.sum(more[WIDE:], axis=0, keepdims=True)


def ring(step):
    return [(i, (i + step) % PARTS) for i in range(PARTS)]


def body(loadings, draws, delta, gamma, pair_rows, pair_cols, pair_count):
    columns = draws.shape[1]
    depth = loadings.shape[1]
    left = lax.ppermute(draws, "scn", ring(2))
    right = lax.ppermute(draws, "scn", ring(-2))
    far = lax.ppermute(draws, "scn", ring(4))
    outgoing, table = pl.pallas_call(
        pick_kernel,
        out_shape=(
            pltpu.VMEM((2 * OWNERS, SLICE, depth), BF16),
            jax.ShapeDtypeStruct((3 * CAP,), jnp.int32),
        ),
        in_specs=[HBM, HBM, HBM, HBM],
        out_specs=(VMEM, SMEM),
        scratch_shapes=[
            pltpu.VMEM((4, LANES), jnp.int32),
            pltpu.VMEM((4, LANES), jnp.int32),
            pltpu.SMEM((4, LANES), jnp.int32),
            pltpu.SMEM((4, LANES), jnp.int32),
            pltpu.SMEM((OWNERS,), jnp.int32),
            pltpu.VMEM((8, LANES), jnp.int32),
            pltpu.SMEM((8, LANES), jnp.int32),
            pltpu.SMEM((OWNERS,), jnp.int32),
            pltpu.SemaphoreType.DMA((2 * OWNERS,)),
            pltpu.SemaphoreType.DMA((6,)),
        ],
        compiler_params=GRANT,
        name="pick",
    )(
        away(pair_rows.reshape(4, LANES)),
        away(pair_cols.reshape(4, LANES)),
        away(pair_count),
        away(loadings),
    )
    arrived = lax.all_to_all(outgoing, "fac", split_axis=0, concat_axis=0, tiled=True)
    chip = lax.axis_index("scn") // 2
    quarter = loadings.shape[0] // (PARTS // 2)
    some = lax.dynamic_slice_in_dim(loadings, chip * quarter, quarter)
    shares = lax.dynamic_slice_in_dim(delta, chip * quarter, quarter)
    slope = jnp.sum(shares[:, None] * some.astype(F32), axis=0)
    tiles = (TILES, SLICE, LANES)
    keep, send = pl.pallas_call(
        regroup_kernel,
        out_shape=(pltpu.VMEM((CHIPS, *tiles), BF16), pltpu.VMEM((CHIPS, *tiles), BF16)),
        in_specs=[SMEM, VMEM, VMEM],
        out_specs=(VMEM, VMEM),
        compiler_params=GRANT,
        name="regroup",
    )(table, near(arrived), gamma)
    partner = [(i, i ^ 1) for i in range(PARTS)]
    swapped = lax.ppermute(send, "scn", partner)
    chunks = pl.pallas_call(
        merge_kernel,
        out_shape=(pltpu.VMEM((2, *tiles), BF16),) * CHIPS,
        in_specs=[VMEM, VMEM],
        out_specs=(VMEM,) * CHIPS,
        compiler_params=GRANT,
        name="merge",
    )(near(keep), near(swapped))
    moved = [lax.ppermute(chunks[k], "scn", ring(2 * k)) for k in range(1, CHIPS)]
    own = pl.pallas_call(
        pair_kernel,
        out_shape=pltpu.VMEM((3, WIDE, WIDE), F32),
        in_specs=[VMEM] * CHIPS,
        out_specs=VMEM,
        scratch_shapes=[pltpu.VMEM((TILES, PARTS, SLICE, LANES), BF16)],
        compiler_params=GRANT,
        name="pair",
    )(near(chunks[0]), *[near(x) for x in moved])
    other = lax.ppermute(own, "scn", partner)
    spread = pl.pallas_call(
        form_kernel,
        out_shape=(pltpu.VMEM((1, columns), F32),) * CHIPS,
        in_specs=[VMEM] * 7,
        out_specs=(VMEM,) * CHIPS,
        compiler_params=GRANT,
        name="form",
    )(near(own), near(other), draws, near(left), near(right), near(far), slope.reshape(1, depth))
    total = spread[0]
    for k in range(1, CHIPS):
        total = total + lax.ppermute(spread[k], "scn", ring(2 * k))
    mine = jnp.broadcast_to(total[None], (OWNERS, 1, columns))
    every = lax.all_to_all(mine, "fac", split_axis=0, concat_axis=0, tiled=True)
    return jnp.sum(every, axis=0).reshape(-1)


def solution(mesh):
    in_specs = (P("fac", None), P(None, "scn"), P("fac"), P("fac", "scn", None), P(), P(), P())
    out_specs = P("scn")
    return jax.shard_map(body, mesh=mesh, in_specs=in_specs, out_specs=out_specs, check_vma=False)
```

```python
import jax
import jax.numpy as jnp
from jax import lax
from jax.experimental import pallas as pl
from jax.experimental.pallas import tpu as pltpu
from jax.sharding import PartitionSpec as P


F32 = jnp.float32
BF16 = jnp.bfloat16
VMEM = pl.BlockSpec(memory_space=pltpu.VMEM)
SMEM = pl.BlockSpec(memory_space=pltpu.SMEM)
HBM = pl.BlockSpec(memory_space=pltpu.HBM)
GRANT = pltpu.CompilerParams(vmem_limit_bytes=24 * 1024 * 1024)
LANES = 128
OWNERS = 32
PARTS = 8
CAP = 16
BLOCKS_DEV = 48
SLICE = 16
GROUPS = 4
WIDE = 256


def near(x):
    return pltpu.with_memory_space_constraint(x, pltpu.VMEM)


def away(x):
    return pltpu.with_memory_space_constraint(x, pltpu.HBM)


def holder_of(block):
    return (block * 1366) >> 16


def pick_kernel(
    rows, cols, count, loadings, out, table,
    rows_v, cols_v, rows_s, cols_s, count_s, keys_v, keys_s, seen, sems, small,
):
    me = lax.axis_index("fac")
    part = lax.axis_index("scn")
    pairs = ((rows, rows_v), (cols, cols_v), (rows, rows_s), (cols, cols_s), (count, count_s))
    moves = [pltpu.make_async_copy(a, b, small.at[i]) for i, (a, b) in enumerate(pairs)]
    for move in moves:
        move.start()
    moves[0].wait()
    moves[1].wait()
    lane = lax.broadcasted_iota(jnp.int32, rows_v.shape, 1) & (CAP - 1)

    def keyed(blocks, first_slot):
        holder = holder_of(blocks)
        key = (lane + first_slot) * 64 + (blocks - holder * BLOCKS_DEV)
        mine = holder == me
        return jnp.where(mine, key, 1 << 20), jnp.where(mine, -key, 1)

    low_r, high_r = keyed(rows_v[...], 0)
    low_c, high_c = keyed(cols_v[...], CAP)
    keys = jnp.concatenate([jnp.minimum(low_r, low_c), jnp.minimum(high_r, high_c)], axis=0)
    for shift in (1, 2, 4, 8):
        keys = jnp.minimum(keys, pltpu.roll(keys, LANES - shift, 1))
    keys_v[...] = keys
    copy = pltpu.make_async_copy(keys_v, keys_s, small.at[5])
    copy.start()
    copy.wait()

    def fetch(slot, offset):
        start = pl.multiple_of(offset * LANES + part * SLICE, SLICE)
        return pltpu.make_async_copy(loadings.at[pl.ds(start, SLICE), :], out.at[slot], sems.at[slot])

    for o in range(OWNERS):
        row, col = o // 8, (o % 8) * CAP
        fetch(2 * o, jnp.minimum(keys_s[row, col] & 63, BLOCKS_DEV - 1)).start()
        fetch(2 * o + 1, jnp.minimum((-keys_s[4 + row, col]) & 63, BLOCKS_DEV - 1)).start()
    for move in moves[2:]:
        move.wait()
    for h in range(OWNERS):
        seen[h] = 0
    row = me // 8
    col = (me % 8) * CAP
    for t in range(2 * CAP):
        block = rows_s[row, col + t] if t < CAP else cols_s[row, col + t - CAP]
        holder = holder_of(block)
        table[t] = 2 * holder + seen[holder]
        seen[holder] = 1
    live = count_s[me]
    for p in range(CAP):
        weight = jnp.where(rows_s[row, col + p] == cols_s[row, col + p], 1, 2)
        table[2 * CAP + p] = jnp.where(p < live, weight, 0)
    for slot in range(2 * OWNERS):
        fetch(slot, 0).wait()


def regroup_kernel(table, recv, gamma, out):
    for t in range(2 * CAP):
        block = recv[table[t]]
        dest = (t % CAP) // 2
        first = ((t % 2) + 2 * (t // CAP)) * GROUPS
        for g in range(GROUPS):
            out[dest, first + g] = block[:, g * LANES : (g + 1) * LANES]
    for p in range(CAP):
        weight = table[2 * CAP + p].astype(F32)
        out[p // 2, 4 * GROUPS + p % 2] = (gamma[p].astype(F32) * weight).astype(BF16)


def pair_kernel(recv, out, sent):
    def block(b):
        tiles = [recv[:, b * GROUPS + g].reshape(LANES, LANES) for g in range(GROUPS)]
        return jnp.concatenate(tiles, axis=1)

    left = []
    high = []
    low = []
    for q in range(2):
        stored = recv[:, 4 * GROUPS + q].reshape(LANES, LANES)
        half = jnp.dot(stored, block(2 + q), preferred_element_type=F32)
        top = half.astype(BF16)
        left.append(block(q))
        high.append(top)
        low.append((half - top.astype(F32)).astype(BF16))
    a = jnp.concatenate(left, axis=0)
    y = jnp.concatenate(high, axis=0)
    z = jnp.concatenate(low, axis=0)
    turned = jnp.concatenate([a.T, a.T, y.T, z.T], axis=1)
    other = jnp.concatenate([y, z, a, a], axis=0)
    out[0] = 0.25 * jnp.dot(turned[:WIDE], other[:, :WIDE], preferred_element_type=F32)
    right = jnp.dot(turned, other[:, WIDE:], preferred_element_type=F32)
    out[1] = 0.5 * right[:WIDE]
    out[2] = 0.25 * right[WIDE:]
    for k in range(3):
        sent[k] = out[k].astype(BF16)


def form_kernel(own, other, here, left, right, far_top, far_low, slope, out):
    chip = lax.axis_index("scn") // 2
    v = slope[...]
    one = v.astype(BF16)
    v = v - one.astype(F32)
    two = v.astype(BF16)
    v = v - two.astype(F32)
    fill = jnp.zeros((13, v.shape[1]), BF16)
    parts = jnp.concatenate([one, two, v.astype(BF16), fill], axis=0)
    first = (own[0] + other[0].astype(F32)).astype(BF16)
    cross = (own[1] + other[1].astype(F32)).astype(BF16)
    last = (own[2] + other[2].astype(F32)).astype(BF16)
    top = jnp.concatenate([first, parts[:, :WIDE]], axis=0)
    low = jnp.concatenate([cross, parts[:, WIDE:], last], axis=0)
    extra = WIDE + parts.shape[0]
    for step, group in enumerate((here, right, None, left)):
        upper = far_top[...] if group is None else group[:WIDE, :]
        lower = far_low[...] if group is None else group[WIDE:, :]
        image = jnp.dot(low, lower, preferred_element_type=F32)
        more = image[:extra] + jnp.dot(top, upper, preferred_element_type=F32)
        total = jnp.sum(more[:WIDE] * upper.astype(F32) + image[extra:] * lower.astype(F32), axis=0, keepdims=True)
        out[(chip + step) & 3] = total + jnp.sum(more[WIDE:], axis=0, keepdims=True)


def ring(step):
    return [(i, (i + step) % PARTS) for i in range(PARTS)]


def body(loadings, draws, delta, gamma, pair_rows, pair_cols, pair_count):
    columns = draws.shape[1]
    depth = loadings.shape[1]
    left = lax.ppermute(draws, "scn", ring(2))
    right = lax.ppermute(draws, "scn", ring(-2))
    far_top = lax.ppermute(left[: depth // 2], "scn", ring(2))
    far_low = lax.ppermute(right[depth // 2 :], "scn", ring(-2))
    outgoing, table = pl.pallas_call(
        pick_kernel,
        out_shape=(
            pltpu.VMEM((2 * OWNERS, SLICE, depth), BF16),
            jax.ShapeDtypeStruct((3 * CAP,), jnp.int32),
        ),
        in_specs=[HBM, HBM, HBM, HBM],
        out_specs=(VMEM, SMEM),
        scratch_shapes=[
            pltpu.VMEM((4, LANES), jnp.int32),
            pltpu.VMEM((4, LANES), jnp.int32),
            pltpu.SMEM((4, LANES), jnp.int32),
            pltpu.SMEM((4, LANES), jnp.int32),
            pltpu.SMEM((OWNERS,), jnp.int32),
            pltpu.VMEM((8, LANES), jnp.int32),
            pltpu.SMEM((8, LANES), jnp.int32),
            pltpu.SMEM((OWNERS,), jnp.int32),
            pltpu.SemaphoreType.DMA((2 * OWNERS,)),
            pltpu.SemaphoreType.DMA((6,)),
        ],
        compiler_params=GRANT,
        name="pick",
    )(
        away(pair_rows.reshape(4, LANES)),
        away(pair_cols.reshape(4, LANES)),
        away(pair_count),
        away(loadings),
    )
    arrived = lax.all_to_all(outgoing, "fac", split_axis=0, concat_axis=0, tiled=True)
    chip = lax.axis_index("scn") // 2
    quarter = loadings.shape[0] // (PARTS // 2)
    some = lax.dynamic_slice_in_dim(loadings, chip * quarter, quarter)
    shares = lax.dynamic_slice_in_dim(delta, chip * quarter, quarter)
    slope = jnp.sum(shares[:, None] * some.astype(F32), axis=0)
    grouped = pl.pallas_call(
        regroup_kernel,
        out_shape=pltpu.VMEM((PARTS, 18, SLICE, LANES), BF16),
        in_specs=[SMEM, VMEM, VMEM],
        out_specs=VMEM,
        compiler_params=GRANT,
        name="regroup",
    )(table, near(arrived), gamma)
    pairs = lax.all_to_all(grouped, "scn", split_axis=0, concat_axis=0, tiled=True)
    own, sent = pl.pallas_call(
        pair_kernel,
        out_shape=(pltpu.VMEM((3, WIDE, WIDE), F32), pltpu.VMEM((3, WIDE, WIDE), BF16)),
        in_specs=[VMEM],
        out_specs=(VMEM, VMEM),
        compiler_params=GRANT,
        name="pair",
    )(near(pairs))
    other = lax.ppermute(sent, "scn", [(i, i ^ 1) for i in range(PARTS)])
    spread = pl.pallas_call(
        form_kernel,
        out_shape=pltpu.VMEM((PARTS // 2, 1, columns), F32),
        in_specs=[VMEM] * 8,
        out_specs=VMEM,
        compiler_params=GRANT,
        name="form",
    )(near(own), near(other), draws, near(left), near(right), near(far_top), near(far_low), slope.reshape(1, depth))
    chips = [[c + 2 * x for x in range(PARTS // 2)] for c in range(2)]
    along = lax.all_to_all(
        spread, "scn", split_axis=0, concat_axis=0, tiled=True, axis_index_groups=chips
    )
    mine = jnp.broadcast_to(jnp.sum(along, axis=0)[None], (OWNERS, 1, columns))
    every = lax.all_to_all(mine, "fac", split_axis=0, concat_axis=0, tiled=True)
    return jnp.sum(every, axis=0).reshape(-1)


def solution(mesh):
    in_specs = (P("fac", None), P(None, "scn"), P("fac"), P("fac", "scn", None), P(), P(), P())
    out_specs = P("scn")
    return jax.shard_map(body, mesh=mesh, in_specs=in_specs, out_specs=out_specs, check_vma=False)
```

```python
import jax
import jax.numpy as jnp
from jax import lax
from jax.experimental import pallas as pl
from jax.experimental.pallas import tpu as pltpu
from jax.sharding import PartitionSpec as P


F32 = jnp.float32
BF16 = jnp.bfloat16
VMEM = pl.BlockSpec(memory_space=pltpu.VMEM)
SMEM = pl.BlockSpec(memory_space=pltpu.SMEM)
HBM = pl.BlockSpec(memory_space=pltpu.HBM)
GRANT = pltpu.CompilerParams(vmem_limit_bytes=24 * 1024 * 1024)
LANES = 128
OWNERS = 32
PARTS = 8
CAP = 16
BLOCKS_DEV = 48
SLICE = 16
GROUPS = 4
WIDE = 256


def near(x):
    return pltpu.with_memory_space_constraint(x, pltpu.VMEM)


def away(x):
    return pltpu.with_memory_space_constraint(x, pltpu.HBM)


def holder_of(block):
    return (block * 1366) >> 16


def pick_kernel(
    rows, cols, count, loadings, out, table,
    rows_v, cols_v, rows_s, cols_s, count_s, keys_v, keys_s, seen, sems, small,
):
    me = lax.axis_index("fac")
    part = lax.axis_index("scn")
    pairs = ((rows, rows_v), (cols, cols_v), (rows, rows_s), (cols, cols_s), (count, count_s))
    moves = [pltpu.make_async_copy(a, b, small.at[i]) for i, (a, b) in enumerate(pairs)]
    for move in moves:
        move.start()
    moves[0].wait()
    moves[1].wait()
    lane = lax.broadcasted_iota(jnp.int32, rows_v.shape, 1) & (CAP - 1)

    def keyed(blocks, first_slot):
        holder = holder_of(blocks)
        key = (lane + first_slot) * 64 + (blocks - holder * BLOCKS_DEV)
        mine = holder == me
        return jnp.where(mine, key, 1 << 20), jnp.where(mine, -key, 1)

    low_r, high_r = keyed(rows_v[...], 0)
    low_c, high_c = keyed(cols_v[...], CAP)
    keys = jnp.concatenate([jnp.minimum(low_r, low_c), jnp.minimum(high_r, high_c)], axis=0)
    for shift in (1, 2, 4, 8):
        keys = jnp.minimum(keys, pltpu.roll(keys, LANES - shift, 1))
    keys_v[...] = keys
    copy = pltpu.make_async_copy(keys_v, keys_s, small.at[5])
    copy.start()
    copy.wait()

    def fetch(slot, offset):
        start = pl.multiple_of(offset * LANES + part * SLICE, SLICE)
        return pltpu.make_async_copy(loadings.at[pl.ds(start, SLICE), :], out.at[slot], sems.at[slot])

    for o in range(OWNERS):
        row, col = o // 8, (o % 8) * CAP
        fetch(2 * o, jnp.minimum(keys_s[row, col] & 63, BLOCKS_DEV - 1)).start()
        fetch(2 * o + 1, jnp.minimum((-keys_s[4 + row, col]) & 63, BLOCKS_DEV - 1)).start()
    for move in moves[2:]:
        move.wait()
    for h in range(OWNERS):
        seen[h] = 0
    row = me // 8
    col = (me % 8) * CAP
    for t in range(2 * CAP):
        block = rows_s[row, col + t] if t < CAP else cols_s[row, col + t - CAP]
        holder = holder_of(block)
        table[t] = 2 * holder + seen[holder]
        seen[holder] = 1
    live = count_s[me]
    for p in range(CAP):
        weight = jnp.where(rows_s[row, col + p] == cols_s[row, col + p], 1, 2)
        table[2 * CAP + p] = jnp.where(p < live, weight, 0)
    for slot in range(2 * OWNERS):
        fetch(slot, 0).wait()


def regroup_kernel(table, recv, gamma, out):
    for t in range(2 * CAP):
        block = recv[table[t]]
        dest = (t % CAP) // 2
        first = ((t % 2) + 2 * (t // CAP)) * GROUPS
        for g in range(GROUPS):
            out[dest, first + g] = block[:, g * LANES : (g + 1) * LANES]
    for p in range(CAP):
        weight = table[2 * CAP + p].astype(F32)
        out[p // 2, 4 * GROUPS + p % 2] = (gamma[p].astype(F32) * weight).astype(BF16)


def pair_kernel(recv, out, sent):
    def block(b):
        tiles = [recv[:, b * GROUPS + g].reshape(LANES, LANES) for g in range(GROUPS)]
        return jnp.concatenate(tiles, axis=1)

    left = []
    high = []
    low = []
    for q in range(2):
        stored = recv[:, 4 * GROUPS + q].reshape(LANES, LANES)
        half = jnp.dot(stored, block(2 + q), preferred_element_type=F32)
        top = half.astype(BF16)
        left.append(block(q))
        high.append(top)
        low.append((half - top.astype(F32)).astype(BF16))
    a = jnp.concatenate(left, axis=0)
    y = jnp.concatenate(high, axis=0)
    z = jnp.concatenate(low, axis=0)
    turned = jnp.concatenate([a.T, a.T, y.T, z.T], axis=1)
    other = jnp.concatenate([y, z, a, a], axis=0)
    out[0] = 0.25 * jnp.dot(turned[:WIDE], other[:, :WIDE], preferred_element_type=F32)
    right = jnp.dot(turned, other[:, WIDE:], preferred_element_type=F32)
    out[1] = 0.5 * right[:WIDE]
    out[2] = 0.25 * right[WIDE:]
    for k in range(3):
        sent[k] = out[k].astype(BF16)


def form_kernel(own, other, here, left, right, top_far, low_far, slope, out, far_top, far_low, sems):
    first_half = pltpu.make_async_copy(top_far, far_top, sems.at[0])
    second_half = pltpu.make_async_copy(low_far, far_low, sems.at[1])
    first_half.start()
    second_half.start()
    chip = lax.axis_index("scn") // 2
    v = slope[...]
    one = v.astype(BF16)
    v = v - one.astype(F32)
    two = v.astype(BF16)
    v = v - two.astype(F32)
    fill = jnp.zeros((13, v.shape[1]), BF16)
    parts = jnp.concatenate([one, two, v.astype(BF16), fill], axis=0)
    first = (own[0] + other[0].astype(F32)).astype(BF16)
    cross = (own[1] + other[1].astype(F32)).astype(BF16)
    last = (own[2] + other[2].astype(F32)).astype(BF16)
    top = jnp.concatenate([first, parts[:, :WIDE]], axis=0)
    low = jnp.concatenate([cross, parts[:, WIDE:], last], axis=0)
    extra = WIDE + parts.shape[0]
    for step, group in ((0, here), (1, right), (3, left), (2, None)):
        if group is None:
            first_half.wait()
            second_half.wait()
        upper = far_top[...] if group is None else group[:WIDE, :]
        lower = far_low[...] if group is None else group[WIDE:, :]
        image = jnp.dot(low, lower, preferred_element_type=F32)
        more = image[:extra] + jnp.dot(top, upper, preferred_element_type=F32)
        total = jnp.sum(more[:WIDE] * upper.astype(F32) + image[extra:] * lower.astype(F32), axis=0, keepdims=True)
        out[(chip + step) & 3] = total + jnp.sum(more[WIDE:], axis=0, keepdims=True)


def ring(step):
    return [(i, (i + step) % PARTS) for i in range(PARTS)]


def body(loadings, draws, delta, gamma, pair_rows, pair_cols, pair_count):
    columns = draws.shape[1]
    depth = loadings.shape[1]
    left = lax.ppermute(draws, "scn", ring(2))
    right = lax.ppermute(draws, "scn", ring(-2))
    far_top = lax.ppermute(left[: depth // 2], "scn", ring(2))
    far_low = lax.ppermute(right[depth // 2 :], "scn", ring(-2))
    outgoing, table = pl.pallas_call(
        pick_kernel,
        out_shape=(
            pltpu.VMEM((2 * OWNERS, SLICE, depth), BF16),
            jax.ShapeDtypeStruct((3 * CAP,), jnp.int32),
        ),
        in_specs=[HBM, HBM, HBM, HBM],
        out_specs=(VMEM, SMEM),
        scratch_shapes=[
            pltpu.VMEM((4, LANES), jnp.int32),
            pltpu.VMEM((4, LANES), jnp.int32),
            pltpu.SMEM((4, LANES), jnp.int32),
            pltpu.SMEM((4, LANES), jnp.int32),
            pltpu.SMEM((OWNERS,), jnp.int32),
            pltpu.VMEM((8, LANES), jnp.int32),
            pltpu.SMEM((8, LANES), jnp.int32),
            pltpu.SMEM((OWNERS,), jnp.int32),
            pltpu.SemaphoreType.DMA((2 * OWNERS,)),
            pltpu.SemaphoreType.DMA((6,)),
        ],
        compiler_params=GRANT,
        name="pick",
    )(
        away(pair_rows.reshape(4, LANES)),
        away(pair_cols.reshape(4, LANES)),
        away(pair_count),
        away(loadings),
    )
    arrived = lax.all_to_all(outgoing, "fac", split_axis=0, concat_axis=0, tiled=True)
    chip = lax.axis_index("scn") // 2
    quarter = loadings.shape[0] // (PARTS // 2)
    some = lax.dynamic_slice_in_dim(loadings, chip * quarter, quarter)
    shares = lax.dynamic_slice_in_dim(delta, chip * quarter, quarter)
    slope = jnp.sum(shares[:, None] * some.astype(F32), axis=0)
    grouped = pl.pallas_call(
        regroup_kernel,
        out_shape=pltpu.VMEM((PARTS, 18, SLICE, LANES), BF16),
        in_specs=[SMEM, VMEM, VMEM],
        out_specs=VMEM,
        compiler_params=GRANT,
        name="regroup",
    )(table, near(arrived), gamma)
    pairs = lax.all_to_all(grouped, "scn", split_axis=0, concat_axis=0, tiled=True)
    own, sent = pl.pallas_call(
        pair_kernel,
        out_shape=(pltpu.VMEM((3, WIDE, WIDE), F32), pltpu.VMEM((3, WIDE, WIDE), BF16)),
        in_specs=[VMEM],
        out_specs=(VMEM, VMEM),
        compiler_params=GRANT,
        name="pair",
    )(near(pairs))
    other = lax.ppermute(sent, "scn", [(i, i ^ 1) for i in range(PARTS)])
    spread = pl.pallas_call(
        form_kernel,
        out_shape=pltpu.VMEM((PARTS // 2, 1, columns), F32),
        in_specs=[VMEM] * 5 + [HBM, HBM, VMEM],
        out_specs=VMEM,
        scratch_shapes=[
            pltpu.VMEM((depth // 2, columns), BF16),
            pltpu.VMEM((depth // 2, columns), BF16),
            pltpu.SemaphoreType.DMA((2,)),
        ],
        compiler_params=GRANT,
        name="form",
    )(near(own), near(other), draws, near(left), near(right), away(far_top), away(far_low), slope.reshape(1, depth))
    chips = [[c + 2 * x for x in range(PARTS // 2)] for c in range(2)]
    along = lax.all_to_all(
        spread, "scn", split_axis=0, concat_axis=0, tiled=True, axis_index_groups=chips
    )
    mine = jnp.broadcast_to(jnp.sum(along, axis=0)[None], (OWNERS, 1, columns))
    every = lax.all_to_all(mine, "fac", split_axis=0, concat_axis=0, tiled=True)
    return jnp.sum(every, axis=0).reshape(-1)


def solution(mesh):
    in_specs = (P("fac", None), P(None, "scn"), P("fac"), P("fac", "scn", None), P(), P(), P())
    out_specs = P("scn")
    return jax.shard_map(body, mesh=mesh, in_specs=in_specs, out_specs=out_specs, check_vma=False)
```

```python
import jax
import jax.numpy as jnp
from jax import lax
from jax.experimental import pallas as pl
from jax.experimental.pallas import tpu as pltpu
from jax.sharding import PartitionSpec as P


F32 = jnp.float32
BF16 = jnp.bfloat16
VMEM = pl.BlockSpec(memory_space=pltpu.VMEM)
SMEM = pl.BlockSpec(memory_space=pltpu.SMEM)
HBM = pl.BlockSpec(memory_space=pltpu.HBM)
GRANT = pltpu.CompilerParams(vmem_limit_bytes=24 * 1024 * 1024)
LANES = 128
OWNERS = 32
PARTS = 8
CAP = 16
BLOCKS_DEV = 48
SLICE = 16
GROUPS = 4
WIDE = 256


def near(x):
    return pltpu.with_memory_space_constraint(x, pltpu.VMEM)


def away(x):
    return pltpu.with_memory_space_constraint(x, pltpu.HBM)


def holder_of(block):
    return (block * 1366) >> 16


def pick_kernel(
    rows, cols, count, loadings, out, table,
    rows_v, cols_v, rows_s, cols_s, count_s, keys_v, keys_s, seen, sems, small,
):
    me = lax.axis_index("fac")
    part = lax.axis_index("scn")
    pairs = ((rows, rows_v), (cols, cols_v), (rows, rows_s), (cols, cols_s), (count, count_s))
    moves = [pltpu.make_async_copy(a, b, small.at[i]) for i, (a, b) in enumerate(pairs)]
    for move in moves:
        move.start()
    moves[0].wait()
    moves[1].wait()
    lane = lax.broadcasted_iota(jnp.int32, rows_v.shape, 1) & (CAP - 1)

    def keyed(blocks, first_slot):
        holder = holder_of(blocks)
        key = (lane + first_slot) * 64 + (blocks - holder * BLOCKS_DEV)
        mine = holder == me
        return jnp.where(mine, key, 1 << 20), jnp.where(mine, -key, 1)

    low_r, high_r = keyed(rows_v[...], 0)
    low_c, high_c = keyed(cols_v[...], CAP)
    keys = jnp.concatenate([jnp.minimum(low_r, low_c), jnp.minimum(high_r, high_c)], axis=0)
    for shift in (1, 2, 4, 8):
        keys = jnp.minimum(keys, pltpu.roll(keys, LANES - shift, 1))
    keys_v[...] = keys
    copy = pltpu.make_async_copy(keys_v, keys_s, small.at[5])
    copy.start()
    copy.wait()

    def fetch(slot, offset):
        start = pl.multiple_of(offset * LANES + part * SLICE, SLICE)
        return pltpu.make_async_copy(loadings.at[pl.ds(start, SLICE), :], out.at[slot], sems.at[slot])

    for o in range(OWNERS):
        row, col = o // 8, (o % 8) * CAP
        fetch(2 * o, jnp.minimum(keys_s[row, col] & 63, BLOCKS_DEV - 1)).start()
        fetch(2 * o + 1, jnp.minimum((-keys_s[4 + row, col]) & 63, BLOCKS_DEV - 1)).start()
    for move in moves[2:]:
        move.wait()
    for h in range(OWNERS):
        seen[h] = 0
    row = me // 8
    col = (me % 8) * CAP
    for t in range(2 * CAP):
        block = rows_s[row, col + t] if t < CAP else cols_s[row, col + t - CAP]
        holder = holder_of(block)
        table[t] = 2 * holder + seen[holder]
        seen[holder] = 1
    live = count_s[me]
    for p in range(CAP):
        weight = jnp.where(rows_s[row, col + p] == cols_s[row, col + p], 1, 2)
        table[2 * CAP + p] = jnp.where(p < live, weight, 0)
    for slot in range(2 * OWNERS):
        fetch(slot, 0).wait()


def regroup_kernel(table, recv, gamma, out):
    for t in range(2 * CAP):
        block = recv[table[t]]
        dest = (t % CAP) // 2
        first = ((t % 2) + 2 * (t // CAP)) * GROUPS
        for g in range(GROUPS):
            out[dest, first + g] = block[:, g * LANES : (g + 1) * LANES]
    for p in range(CAP):
        weight = table[2 * CAP + p].astype(F32)
        out[p // 2, 4 * GROUPS + p % 2] = (gamma[p].astype(F32) * weight).astype(BF16)


def pair_kernel(recv, out, sent):
    def block(b):
        tiles = [recv[:, b * GROUPS + g].reshape(LANES, LANES) for g in range(GROUPS)]
        return jnp.concatenate(tiles, axis=1)

    left = []
    high = []
    low = []
    for q in range(2):
        stored = recv[:, 4 * GROUPS + q].reshape(LANES, LANES)
        half = jnp.dot(stored, block(2 + q), preferred_element_type=F32)
        top = half.astype(BF16)
        left.append(block(q))
        high.append(top)
        low.append((half - top.astype(F32)).astype(BF16))
    a = jnp.concatenate(left, axis=0)
    y = jnp.concatenate(high, axis=0)
    z = jnp.concatenate(low, axis=0)
    turned = jnp.concatenate([a.T, a.T, y.T, z.T], axis=1)
    other = jnp.concatenate([y, z, a, a], axis=0)
    out[0] = 0.25 * jnp.dot(turned[:WIDE], other[:, :WIDE], preferred_element_type=F32)
    right = jnp.dot(turned, other[:, WIDE:], preferred_element_type=F32)
    out[1] = 0.5 * right[:WIDE]
    out[2] = 0.25 * right[WIDE:]
    for k in range(3):
        sent[k] = out[k].astype(BF16)


def form_kernel(
    own, other, here, left_top, left_low, right_top, right_low, top_far, low_far, slope, out, far_top, far_low, sems
):
    first_half = pltpu.make_async_copy(top_far, far_top, sems.at[0])
    second_half = pltpu.make_async_copy(low_far, far_low, sems.at[1])
    first_half.start()
    second_half.start()
    chip = lax.axis_index("scn") // 2
    v = slope[...]
    one = v.astype(BF16)
    v = v - one.astype(F32)
    two = v.astype(BF16)
    v = v - two.astype(F32)
    fill = jnp.zeros((13, v.shape[1]), BF16)
    parts = jnp.concatenate([one, two, v.astype(BF16), fill], axis=0)
    first = (own[0] + other[0].astype(F32)).astype(BF16)
    cross = (own[1] + other[1].astype(F32)).astype(BF16)
    last = (own[2] + other[2].astype(F32)).astype(BF16)
    top = jnp.concatenate([first, parts[:, :WIDE]], axis=0)
    low = jnp.concatenate([cross, parts[:, WIDE:], last], axis=0)
    extra = WIDE + parts.shape[0]
    whole = (here.at[:WIDE, :], here.at[WIDE:, :])
    groups = ((0, whole), (1, (right_top, right_low)), (3, (left_top, left_low)), (2, (far_top, far_low)))
    for step, halves in groups:
        if step == 2:
            first_half.wait()
            second_half.wait()
        upper = halves[0][...]
        lower = halves[1][...]
        image = jnp.dot(low, lower, preferred_element_type=F32)
        more = image[:extra] + jnp.dot(top, upper, preferred_element_type=F32)
        total = jnp.sum(more[:WIDE] * upper.astype(F32) + image[extra:] * lower.astype(F32), axis=0, keepdims=True)
        out[(chip + step) & 3] = total + jnp.sum(more[WIDE:], axis=0, keepdims=True)


def ring(step):
    return [(i, (i + step) % PARTS) for i in range(PARTS)]


def body(loadings, draws, delta, gamma, pair_rows, pair_cols, pair_count):
    columns = draws.shape[1]
    depth = loadings.shape[1]
    upper, lower = draws[: depth // 2], draws[depth // 2 :]
    left_top = lax.ppermute(upper, "scn", ring(2))
    right_low = lax.ppermute(lower, "scn", ring(-2))
    left_low = lax.ppermute(lower, "scn", ring(2))
    right_top = lax.ppermute(upper, "scn", ring(-2))
    far_top = lax.ppermute(left_top, "scn", ring(2))
    far_low = lax.ppermute(right_low, "scn", ring(-2))
    outgoing, table = pl.pallas_call(
        pick_kernel,
        out_shape=(
            pltpu.VMEM((2 * OWNERS, SLICE, depth), BF16),
            jax.ShapeDtypeStruct((3 * CAP,), jnp.int32),
        ),
        in_specs=[HBM, HBM, HBM, HBM],
        out_specs=(VMEM, SMEM),
        scratch_shapes=[
            pltpu.VMEM((4, LANES), jnp.int32),
            pltpu.VMEM((4, LANES), jnp.int32),
            pltpu.SMEM((4, LANES), jnp.int32),
            pltpu.SMEM((4, LANES), jnp.int32),
            pltpu.SMEM((OWNERS,), jnp.int32),
            pltpu.VMEM((8, LANES), jnp.int32),
            pltpu.SMEM((8, LANES), jnp.int32),
            pltpu.SMEM((OWNERS,), jnp.int32),
            pltpu.SemaphoreType.DMA((2 * OWNERS,)),
            pltpu.SemaphoreType.DMA((6,)),
        ],
        compiler_params=GRANT,
        name="pick",
    )(
        away(pair_rows.reshape(4, LANES)),
        away(pair_cols.reshape(4, LANES)),
        away(pair_count),
        away(loadings),
    )
    arrived = lax.all_to_all(outgoing, "fac", split_axis=0, concat_axis=0, tiled=True)
    chip = lax.axis_index("scn") // 2
    quarter = loadings.shape[0] // (PARTS // 2)
    some = lax.dynamic_slice_in_dim(loadings, chip * quarter, quarter)
    shares = lax.dynamic_slice_in_dim(delta, chip * quarter, quarter)
    slope = jnp.sum(shares[:, None] * some.astype(F32), axis=0)
    grouped = pl.pallas_call(
        regroup_kernel,
        out_shape=pltpu.VMEM((PARTS, 18, SLICE, LANES), BF16),
        in_specs=[SMEM, VMEM, VMEM],
        out_specs=VMEM,
        compiler_params=GRANT,
        name="regroup",
    )(table, near(arrived), gamma)
    pairs = lax.all_to_all(grouped, "scn", split_axis=0, concat_axis=0, tiled=True)
    own, sent = pl.pallas_call(
        pair_kernel,
        out_shape=(pltpu.VMEM((3, WIDE, WIDE), F32), pltpu.VMEM((3, WIDE, WIDE), BF16)),
        in_specs=[VMEM],
        out_specs=(VMEM, VMEM),
        compiler_params=GRANT,
        name="pair",
    )(near(pairs))
    other = lax.ppermute(sent, "scn", [(i, i ^ 1) for i in range(PARTS)])
    spread = pl.pallas_call(
        form_kernel,
        out_shape=pltpu.VMEM((PARTS // 2, 1, columns), F32),
        in_specs=[VMEM] * 7 + [HBM, HBM, VMEM],
        out_specs=VMEM,
        scratch_shapes=[
            pltpu.VMEM((depth // 2, columns), BF16),
            pltpu.VMEM((depth // 2, columns), BF16),
            pltpu.SemaphoreType.DMA((2,)),
        ],
        compiler_params=GRANT,
        name="form",
    )(near(own), near(other), draws, near(left_top), near(left_low), near(right_top), near(right_low), away(far_top), away(far_low), slope.reshape(1, depth))
    chips = [[c + 2 * x for x in range(PARTS // 2)] for c in range(2)]
    along = lax.all_to_all(
        spread, "scn", split_axis=0, concat_axis=0, tiled=True, axis_index_groups=chips
    )
    mine = jnp.broadcast_to(jnp.sum(along, axis=0)[None], (OWNERS, 1, columns))
    every = lax.all_to_all(mine, "fac", split_axis=0, concat_axis=0, tiled=True)
    return jnp.sum(every, axis=0).reshape(-1)


def solution(mesh):
    in_specs = (P("fac", None), P(None, "scn"), P("fac"), P("fac", "scn", None), P(), P(), P())
    out_specs = P("scn")
    return jax.shard_map(body, mesh=mesh, in_specs=in_specs, out_specs=out_specs, check_vma=False)
```

```python
import jax
import jax.numpy as jnp
from jax import lax
from jax.experimental import pallas as pl
from jax.experimental.pallas import tpu as pltpu
from jax.sharding import PartitionSpec as P


F32 = jnp.float32
BF16 = jnp.bfloat16
VMEM = pl.BlockSpec(memory_space=pltpu.VMEM)
SMEM = pl.BlockSpec(memory_space=pltpu.SMEM)
HBM = pl.BlockSpec(memory_space=pltpu.HBM)
GRANT = pltpu.CompilerParams(vmem_limit_bytes=24 * 1024 * 1024)
LANES = 128
OWNERS = 32
PARTS = 8
CAP = 16
BLOCKS_DEV = 48
SLICE = 16
GROUPS = 4
WIDE = 256


def near(x):
    return pltpu.with_memory_space_constraint(x, pltpu.VMEM)


def away(x):
    return pltpu.with_memory_space_constraint(x, pltpu.HBM)


def holder_of(block):
    return (block * 1366) >> 16


def pick_kernel(
    rows, cols, count, loadings, out, table,
    rows_v, cols_v, rows_s, cols_s, count_s, seen, sems, small,
):
    me = lax.axis_index("fac")
    part = lax.axis_index("scn")
    pairs = ((rows, rows_v), (cols, cols_v), (rows, rows_s), (cols, cols_s), (count, count_s))
    moves = [pltpu.make_async_copy(a, b, small.at[i]) for i, (a, b) in enumerate(pairs)]
    for move in moves:
        move.start()
    moves[0].wait()
    moves[1].wait()
    lane = lax.broadcasted_iota(jnp.int32, rows_v.shape, 1) & (CAP - 1)

    def keyed(blocks, first_slot):
        holder = holder_of(blocks)
        key = (lane + first_slot) * 64 + (blocks - holder * BLOCKS_DEV)
        mine = holder == me
        return jnp.where(mine, key, 1 << 20), jnp.where(mine, -key, 1)

    low_r, high_r = keyed(rows_v[...], 0)
    low_c, high_c = keyed(cols_v[...], CAP)
    keys = jnp.concatenate([jnp.minimum(low_r, low_c), jnp.minimum(high_r, high_c)], axis=0)
    for shift in (1, 2, 4, 8):
        keys = jnp.minimum(keys, pltpu.roll(keys, LANES - shift, 1))

    def fetch(slot, offset):
        start = pl.multiple_of(offset * LANES + part * SLICE, SLICE)
        return pltpu.make_async_copy(loadings.at[pl.ds(start, SLICE), :], out.at[slot], sems.at[slot])

    for o in range(OWNERS):
        row, col = o // 8, (o % 8) * CAP
        fetch(2 * o, jnp.minimum(keys[row, col] & 63, BLOCKS_DEV - 1)).start()
        fetch(2 * o + 1, jnp.minimum((-keys[4 + row, col]) & 63, BLOCKS_DEV - 1)).start()
    for move in moves[2:]:
        move.wait()
    for h in range(OWNERS):
        seen[h] = 0
    row = me // 8
    col = (me % 8) * CAP
    for t in range(2 * CAP):
        block = rows_s[row, col + t] if t < CAP else cols_s[row, col + t - CAP]
        holder = holder_of(block)
        table[t] = 2 * holder + seen[holder]
        seen[holder] = 1
    live = count_s[me]
    for p in range(CAP):
        weight = jnp.where(rows_s[row, col + p] == cols_s[row, col + p], 1, 2)
        table[2 * CAP + p] = jnp.where(p < live, weight, 0)
    for slot in range(2 * OWNERS):
        fetch(slot, 0).wait()


def regroup_kernel(table, recv, gamma, out):
    for t in range(2 * CAP):
        block = recv[table[t]]
        dest = (t % CAP) // 2
        first = ((t % 2) + 2 * (t // CAP)) * GROUPS
        for g in range(GROUPS):
            out[dest, first + g] = block[:, g * LANES : (g + 1) * LANES]
    for p in range(CAP):
        weight = table[2 * CAP + p].astype(F32)
        out[p // 2, 4 * GROUPS + p % 2] = (gamma[p].astype(F32) * weight).astype(BF16)


def pair_kernel(recv, out, sent):
    def block(b):
        tiles = [recv[:, b * GROUPS + g].reshape(LANES, LANES) for g in range(GROUPS)]
        return jnp.concatenate(tiles, axis=1)

    left = []
    high = []
    low = []
    for q in range(2):
        stored = recv[:, 4 * GROUPS + q].reshape(LANES, LANES)
        half = jnp.dot(stored, block(2 + q), preferred_element_type=F32)
        top = half.astype(BF16)
        left.append(block(q))
        high.append(top)
        low.append((half - top.astype(F32)).astype(BF16))
    a = jnp.concatenate(left, axis=0)
    y = jnp.concatenate(high, axis=0)
    z = jnp.concatenate(low, axis=0)
    turned = jnp.concatenate([a.T, a.T, y.T, z.T], axis=1)
    other = jnp.concatenate([y, z, a, a], axis=0)
    out[0] = 0.25 * jnp.dot(turned[:WIDE], other[:, :WIDE], preferred_element_type=F32)
    right = jnp.dot(turned, other[:, WIDE:], preferred_element_type=F32)
    out[1] = 0.5 * right[:WIDE]
    out[2] = 0.25 * right[WIDE:]
    for k in range(3):
        sent[k] = out[k].astype(BF16)


def form_kernel(
    own, other, here, left_top, left_low, right_top, right_low, top_far, low_far, slope, out, far_top, far_low, sems
):
    first_half = pltpu.make_async_copy(top_far, far_top, sems.at[0])
    second_half = pltpu.make_async_copy(low_far, far_low, sems.at[1])
    first_half.start()
    second_half.start()
    chip = lax.axis_index("scn") // 2
    v = slope[...]
    one = v.astype(BF16)
    v = v - one.astype(F32)
    two = v.astype(BF16)
    v = v - two.astype(F32)
    fill = jnp.zeros((13, v.shape[1]), BF16)
    parts = jnp.concatenate([one, two, v.astype(BF16), fill], axis=0)
    first = (own[0] + other[0].astype(F32)).astype(BF16)
    cross = (own[1] + other[1].astype(F32)).astype(BF16)
    last = (own[2] + other[2].astype(F32)).astype(BF16)
    top = jnp.concatenate([first, parts[:, :WIDE]], axis=0)
    low = jnp.concatenate([cross, parts[:, WIDE:], last], axis=0)
    extra = WIDE + parts.shape[0]
    whole = (here.at[:WIDE, :], here.at[WIDE:, :])
    groups = ((0, whole), (1, (right_top, right_low)), (3, (left_top, left_low)), (2, (far_top, far_low)))
    for step, halves in groups:
        if step == 2:
            first_half.wait()
            second_half.wait()
        upper = halves[0][...]
        lower = halves[1][...]
        image = jnp.dot(low, lower, preferred_element_type=F32)
        more = image[:extra] + jnp.dot(top, upper, preferred_element_type=F32)
        total = jnp.sum(more[:WIDE] * upper.astype(F32) + image[extra:] * lower.astype(F32), axis=0, keepdims=True)
        out[(chip + step) & 3] = total + jnp.sum(more[WIDE:], axis=0, keepdims=True)


def ring(step):
    return [(i, (i + step) % PARTS) for i in range(PARTS)]


def body(loadings, draws, delta, gamma, pair_rows, pair_cols, pair_count):
    columns = draws.shape[1]
    depth = loadings.shape[1]
    upper, lower = draws[: depth // 2], draws[depth // 2 :]
    left_top = lax.ppermute(upper, "scn", ring(2))
    right_low = lax.ppermute(lower, "scn", ring(-2))
    left_low = lax.ppermute(lower, "scn", ring(2))
    right_top = lax.ppermute(upper, "scn", ring(-2))
    far_top = lax.ppermute(left_top, "scn", ring(2))
    far_low = lax.ppermute(right_low, "scn", ring(-2))
    outgoing, table = pl.pallas_call(
        pick_kernel,
        out_shape=(
            pltpu.VMEM((2 * OWNERS, SLICE, depth), BF16),
            jax.ShapeDtypeStruct((3 * CAP,), jnp.int32),
        ),
        in_specs=[HBM, HBM, HBM, HBM],
        out_specs=(VMEM, SMEM),
        scratch_shapes=[
            pltpu.VMEM((4, LANES), jnp.int32),
            pltpu.VMEM((4, LANES), jnp.int32),
            pltpu.SMEM((4, LANES), jnp.int32),
            pltpu.SMEM((4, LANES), jnp.int32),
            pltpu.SMEM((OWNERS,), jnp.int32),
            pltpu.SMEM((OWNERS,), jnp.int32),
            pltpu.SemaphoreType.DMA((2 * OWNERS,)),
            pltpu.SemaphoreType.DMA((5,)),
        ],
        compiler_params=GRANT,
        name="pick",
    )(
        away(pair_rows.reshape(4, LANES)),
        away(pair_cols.reshape(4, LANES)),
        away(pair_count),
        away(loadings),
    )
    arrived = lax.all_to_all(outgoing, "fac", split_axis=0, concat_axis=0, tiled=True)
    chip = lax.axis_index("scn") // 2
    quarter = loadings.shape[0] // (PARTS // 2)
    some = lax.dynamic_slice_in_dim(loadings, chip * quarter, quarter)
    shares = lax.dynamic_slice_in_dim(delta, chip * quarter, quarter)
    slope = jnp.sum(shares[:, None] * some.astype(F32), axis=0)
    grouped = pl.pallas_call(
        regroup_kernel,
        out_shape=pltpu.VMEM((PARTS, 18, SLICE, LANES), BF16),
        in_specs=[SMEM, VMEM, VMEM],
        out_specs=VMEM,
        compiler_params=GRANT,
        name="regroup",
    )(table, near(arrived), gamma)
    pairs = lax.all_to_all(grouped, "scn", split_axis=0, concat_axis=0, tiled=True)
    own, sent = pl.pallas_call(
        pair_kernel,
        out_shape=(pltpu.VMEM((3, WIDE, WIDE), F32), pltpu.VMEM((3, WIDE, WIDE), BF16)),
        in_specs=[VMEM],
        out_specs=(VMEM, VMEM),
        compiler_params=GRANT,
        name="pair",
    )(near(pairs))
    other = lax.ppermute(sent, "scn", [(i, i ^ 1) for i in range(PARTS)])
    spread = pl.pallas_call(
        form_kernel,
        out_shape=pltpu.VMEM((PARTS // 2, 1, columns), F32),
        in_specs=[VMEM] * 7 + [HBM, HBM, VMEM],
        out_specs=VMEM,
        scratch_shapes=[
            pltpu.VMEM((depth // 2, columns), BF16),
            pltpu.VMEM((depth // 2, columns), BF16),
            pltpu.SemaphoreType.DMA((2,)),
        ],
        compiler_params=GRANT,
        name="form",
    )(near(own), near(other), draws, near(left_top), near(left_low), near(right_top), near(right_low), away(far_top), away(far_low), slope.reshape(1, depth))
    chips = [[c + 2 * x for x in range(PARTS // 2)] for c in range(2)]
    along = lax.all_to_all(
        spread, "scn", split_axis=0, concat_axis=0, tiled=True, axis_index_groups=chips
    )
    mine = jnp.broadcast_to(jnp.sum(along, axis=0)[None], (OWNERS, 1, columns))
    every = lax.all_to_all(mine, "fac", split_axis=0, concat_axis=0, tiled=True)
    return jnp.sum(every, axis=0).reshape(-1)


def solution(mesh):
    in_specs = (P("fac", None), P(None, "scn"), P("fac"), P("fac", "scn", None), P(), P(), P())
    out_specs = P("scn")
    return jax.shard_map(body, mesh=mesh, in_specs=in_specs, out_specs=out_specs, check_vma=False)
```

```python
import jax
import jax.numpy as jnp
from jax import lax
from jax.experimental import pallas as pl
from jax.experimental.pallas import tpu as pltpu
from jax.sharding import PartitionSpec as P


F32 = jnp.float32
BF16 = jnp.bfloat16
VMEM = pl.BlockSpec(memory_space=pltpu.VMEM)
SMEM = pl.BlockSpec(memory_space=pltpu.SMEM)
HBM = pl.BlockSpec(memory_space=pltpu.HBM)
GRANT = pltpu.CompilerParams(vmem_limit_bytes=24 * 1024 * 1024)
LANES = 128
OWNERS = 32
PARTS = 8
CAP = 16
BLOCKS_DEV = 48
SLICE = 16
GROUPS = 4
WIDE = 256


def near(x):
    return pltpu.with_memory_space_constraint(x, pltpu.VMEM)


def away(x):
    return pltpu.with_memory_space_constraint(x, pltpu.HBM)


def holder_of(block):
    return (block * 1366) >> 16


def pick_kernel(
    rows, cols, count, loadings, out, table,
    rows_v, cols_v, rows_s, cols_s, count_s, seen, sems, small,
):
    me = lax.axis_index("fac")
    part = lax.axis_index("scn")
    pairs = ((rows, rows_v), (cols, cols_v), (rows, rows_s), (cols, cols_s), (count, count_s))
    moves = [pltpu.make_async_copy(a, b, small.at[i]) for i, (a, b) in enumerate(pairs)]
    for move in moves:
        move.start()
    moves[0].wait()
    moves[1].wait()
    lane = lax.broadcasted_iota(jnp.int32, rows_v.shape, 1) & (CAP - 1)

    def keyed(blocks, first_slot):
        holder = holder_of(blocks)
        key = (lane + first_slot) * 64 + (blocks - holder * BLOCKS_DEV)
        mine = holder == me
        return jnp.where(mine, key, 1 << 20), jnp.where(mine, -key, 1)

    low_r, high_r = keyed(rows_v[...], 0)
    low_c, high_c = keyed(cols_v[...], CAP)
    keys = jnp.concatenate([jnp.minimum(low_r, low_c), jnp.minimum(high_r, high_c)], axis=0)
    for shift in (1, 2, 4, 8):
        keys = jnp.minimum(keys, pltpu.roll(keys, LANES - shift, 1))

    def fetch(slot, offset):
        start = pl.multiple_of(offset * LANES + part * SLICE, SLICE)
        return pltpu.make_async_copy(loadings.at[pl.ds(start, SLICE), :], out.at[slot], sems.at[slot])

    for o in range(OWNERS):
        row, col = o // 8, (o % 8) * CAP
        fetch(2 * o, jnp.minimum(keys[row, col] & 63, BLOCKS_DEV - 1)).start()
        fetch(2 * o + 1, jnp.minimum((-keys[4 + row, col]) & 63, BLOCKS_DEV - 1)).start()
    for move in moves[2:]:
        move.wait()
    for h in range(OWNERS):
        seen[h] = 0
    row = me // 8
    col = (me % 8) * CAP
    for t in range(2 * CAP):
        block = rows_s[row, col + t] if t < CAP else cols_s[row, col + t - CAP]
        holder = holder_of(block)
        table[t] = 2 * holder + seen[holder]
        seen[holder] = 1
    live = count_s[me]
    for p in range(CAP):
        weight = jnp.where(rows_s[row, col + p] == cols_s[row, col + p], 1, 2)
        table[2 * CAP + p] = jnp.where(p < live, weight, 0)
    for slot in range(2 * OWNERS):
        fetch(slot, 0).wait()


def regroup_kernel(table, recv, gamma, out):
    for t in range(2 * CAP):
        block = recv[table[t]]
        dest = (t % CAP) // 2
        first = ((t % 2) + 2 * (t // CAP)) * GROUPS
        for g in range(GROUPS):
            out[dest, first + g] = block[:, g * LANES : (g + 1) * LANES]
    for p in range(CAP):
        weight = table[2 * CAP + p].astype(F32)
        out[p // 2, 4 * GROUPS + p % 2] = (gamma[p].astype(F32) * weight).astype(BF16)


def pair_kernel(recv, out, sent):
    def block(b):
        tiles = [recv[:, b * GROUPS + g].reshape(LANES, LANES) for g in range(GROUPS)]
        return jnp.concatenate(tiles, axis=1)

    left = []
    high = []
    low = []
    for q in range(2):
        stored = recv[:, 4 * GROUPS + q].reshape(LANES, LANES)
        half = jnp.dot(stored, block(2 + q), preferred_element_type=F32)
        top = half.astype(BF16)
        left.append(block(q))
        high.append(top)
        low.append((half - top.astype(F32)).astype(BF16))
    a = jnp.concatenate(left, axis=0)
    y = jnp.concatenate(high, axis=0)
    z = jnp.concatenate(low, axis=0)
    turned = jnp.concatenate([a.T, a.T, y.T, z.T], axis=1)
    other = jnp.concatenate([y, z, a, a], axis=0)
    out[0] = 0.25 * jnp.dot(turned[:WIDE], other[:, :WIDE], preferred_element_type=F32)
    right = jnp.dot(turned, other[:, WIDE:], preferred_element_type=F32)
    out[1] = 0.5 * right[:WIDE]
    out[2] = 0.25 * right[WIDE:]
    for k in range(3):
        sent[k] = out[k].astype(BF16)


def form_kernel(
    own, other, here, left_top, left_low, right_top, right_low, top_far, low_far, slope,
    mine, across, sent, out, far_top, far_low, sems,
):
    first_half = pltpu.make_async_copy(top_far, far_top, sems.at[0])
    second_half = pltpu.make_async_copy(low_far, far_low, sems.at[1])
    first_half.start()
    second_half.start()
    chip = lax.axis_index("scn") // 2
    v = slope[...]
    one = v.astype(BF16)
    v = v - one.astype(F32)
    two = v.astype(BF16)
    v = v - two.astype(F32)
    fill = jnp.zeros((13, v.shape[1]), BF16)
    parts = jnp.concatenate([one, two, v.astype(BF16), fill], axis=0)
    first = (own[0] + other[0].astype(F32)).astype(BF16)
    cross = (own[1] + other[1].astype(F32)).astype(BF16)
    last = (own[2] + other[2].astype(F32)).astype(BF16)
    top = jnp.concatenate([first, parts[:, :WIDE]], axis=0)
    low = jnp.concatenate([cross, parts[:, WIDE:], last], axis=0)
    extra = WIDE + parts.shape[0]
    whole = (here.at[:WIDE, :], here.at[WIDE:, :])
    groups = ((0, whole), (1, (right_top, right_low)), (3, (left_top, left_low)), (2, (far_top, far_low)))
    for step, halves in groups:
        if step == 2:
            first_half.wait()
            second_half.wait()
        upper = halves[0][...]
        lower = halves[1][...]
        image = jnp.dot(low, lower, preferred_element_type=F32)
        more = image[:extra] + jnp.dot(top, upper, preferred_element_type=F32)
        total = jnp.sum(more[:WIDE] * upper.astype(F32) + image[extra:] * lower.astype(F32), axis=0, keepdims=True)
        group = (chip + step) & 3
        beside = group == (chip ^ 1)
        place = jnp.where(group == 3 - chip, 1, jnp.where(beside, 2, 3)) if step else 0
        out[place] = total + jnp.sum(more[WIDE:], axis=0, keepdims=True)
    mine[...] = out[0]
    across[...] = out[1]
    sent[0] = out[2]
    sent[1] = out[3]


def ring(step):
    return [(i, (i + step) % PARTS) for i in range(PARTS)]


def body(loadings, draws, delta, gamma, pair_rows, pair_cols, pair_count):
    columns = draws.shape[1]
    depth = loadings.shape[1]
    upper, lower = draws[: depth // 2], draws[depth // 2 :]
    left_top = lax.ppermute(upper, "scn", ring(2))
    right_low = lax.ppermute(lower, "scn", ring(-2))
    left_low = lax.ppermute(lower, "scn", ring(2))
    right_top = lax.ppermute(upper, "scn", ring(-2))
    far_top = lax.ppermute(left_top, "scn", ring(2))
    far_low = lax.ppermute(right_low, "scn", ring(-2))
    outgoing, table = pl.pallas_call(
        pick_kernel,
        out_shape=(
            pltpu.VMEM((2 * OWNERS, SLICE, depth), BF16),
            jax.ShapeDtypeStruct((3 * CAP,), jnp.int32),
        ),
        in_specs=[HBM, HBM, HBM, HBM],
        out_specs=(VMEM, SMEM),
        scratch_shapes=[
            pltpu.VMEM((4, LANES), jnp.int32),
            pltpu.VMEM((4, LANES), jnp.int32),
            pltpu.SMEM((4, LANES), jnp.int32),
            pltpu.SMEM((4, LANES), jnp.int32),
            pltpu.SMEM((OWNERS,), jnp.int32),
            pltpu.SMEM((OWNERS,), jnp.int32),
            pltpu.SemaphoreType.DMA((2 * OWNERS,)),
            pltpu.SemaphoreType.DMA((5,)),
        ],
        compiler_params=GRANT,
        name="pick",
    )(
        away(pair_rows.reshape(4, LANES)),
        away(pair_cols.reshape(4, LANES)),
        away(pair_count),
        away(loadings),
    )
    arrived = lax.all_to_all(outgoing, "fac", split_axis=0, concat_axis=0, tiled=True)
    chip = lax.axis_index("scn") // 2
    quarter = loadings.shape[0] // (PARTS // 2)
    some = lax.dynamic_slice_in_dim(loadings, chip * quarter, quarter)
    shares = lax.dynamic_slice_in_dim(delta, chip * quarter, quarter)
    slope = jnp.sum(shares[:, None] * some.astype(F32), axis=0)
    grouped = pl.pallas_call(
        regroup_kernel,
        out_shape=pltpu.VMEM((PARTS, 18, SLICE, LANES), BF16),
        in_specs=[SMEM, VMEM, VMEM],
        out_specs=VMEM,
        compiler_params=GRANT,
        name="regroup",
    )(table, near(arrived), gamma)
    pairs = lax.all_to_all(grouped, "scn", split_axis=0, concat_axis=0, tiled=True)
    own, sent = pl.pallas_call(
        pair_kernel,
        out_shape=(pltpu.VMEM((3, WIDE, WIDE), F32), pltpu.VMEM((3, WIDE, WIDE), BF16)),
        in_specs=[VMEM],
        out_specs=(VMEM, VMEM),
        compiler_params=GRANT,
        name="pair",
    )(near(pairs))
    other = lax.ppermute(sent, "scn", [(i, i ^ 1) for i in range(PARTS)])
    mine, across, send = pl.pallas_call(
        form_kernel,
        out_shape=(
            pltpu.VMEM((1, columns), F32),
            pltpu.VMEM((1, columns), F32),
            pltpu.VMEM((2, 1, columns), F32),
        ),
        in_specs=[VMEM] * 7 + [HBM, HBM, VMEM],
        out_specs=(VMEM, VMEM, VMEM),
        scratch_shapes=[
            pltpu.VMEM((4, 1, columns), F32),
            pltpu.VMEM((depth // 2, columns), BF16),
            pltpu.VMEM((depth // 2, columns), BF16),
            pltpu.SemaphoreType.DMA((2,)),
        ],
        compiler_params=GRANT,
        name="form",
    )(near(own), near(other), draws, near(left_top), near(left_low), near(right_top), near(right_low), away(far_top), away(far_low), slope.reshape(1, depth))
    near_sum = lax.ppermute(send, "scn", [(i, i ^ 2) for i in range(PARTS)])
    across = across + near_sum[1]
    over = lax.ppermute(across, "scn", [(i, 6 - i + 2 * (i % 2)) for i in range(PARTS)])
    total = mine + near_sum[0] + over
    spread = jnp.broadcast_to(total[None], (OWNERS, 1, columns))
    every = lax.all_to_all(spread, "fac", split_axis=0, concat_axis=0, tiled=True)
    return jnp.sum(every, axis=0).reshape(-1)


def solution(mesh):
    in_specs = (P("fac", None), P(None, "scn"), P("fac"), P("fac", "scn", None), P(), P(), P())
    out_specs = P("scn")
    return jax.shard_map(body, mesh=mesh, in_specs=in_specs, out_specs=out_specs, check_vma=False)
```

```python
import functools

import jax
import jax.numpy as jnp
from jax import lax
from jax.experimental import pallas as pl
from jax.experimental.pallas import tpu as pltpu
from jax.sharding import PartitionSpec as P


F32 = jnp.float32
BF16 = jnp.bfloat16
VMEM = pl.BlockSpec(memory_space=pltpu.VMEM)
SMEM = pl.BlockSpec(memory_space=pltpu.SMEM)
HBM = pl.BlockSpec(memory_space=pltpu.HBM)
GRANT = pltpu.CompilerParams(vmem_limit_bytes=24 * 1024 * 1024)
LANES = 128
OWNERS = 32
PARTS = 8
CAP = 16
BLOCKS_DEV = 48
SLICE = 16
GROUPS = 4
WIDE = 256


def near(x):
    return pltpu.with_memory_space_constraint(x, pltpu.VMEM)


def away(x):
    return pltpu.with_memory_space_constraint(x, pltpu.HBM)


def holder_of(block):
    return (block * 1366) >> 16


def pick_kernel(
    rows, cols, count, loadings, out, table,
    rows_v, cols_v, rows_s, cols_s, count_s, seen, held, sems, out_sems, small,
):
    me = lax.axis_index("fac")
    part = lax.axis_index("scn")
    pairs = ((rows, rows_v), (cols, cols_v), (rows, rows_s), (cols, cols_s), (count, count_s))
    moves = [pltpu.make_async_copy(a, b, small.at[i]) for i, (a, b) in enumerate(pairs)]
    for move in moves:
        move.start()
    moves[0].wait()
    moves[1].wait()
    lane = lax.broadcasted_iota(jnp.int32, rows_v.shape, 1) & (CAP - 1)

    def keyed(blocks, first_slot):
        holder = holder_of(blocks)
        key = (lane + first_slot) * 64 + (blocks - holder * BLOCKS_DEV)
        mine = holder == me
        return jnp.where(mine, key, 1 << 20), jnp.where(mine, -key, 1)

    low_r, high_r = keyed(rows_v[...], 0)
    low_c, high_c = keyed(cols_v[...], CAP)
    keys = jnp.concatenate([jnp.minimum(low_r, low_c), jnp.minimum(high_r, high_c)], axis=0)
    for shift in (1, 2, 4, 8):
        keys = jnp.minimum(keys, pltpu.roll(keys, LANES - shift, 1))

    def fetch(slot, offset):
        start = pl.multiple_of(offset * LANES + part * SLICE, SLICE)
        return pltpu.make_async_copy(loadings.at[pl.ds(start, SLICE), :], held.at[slot], sems.at[slot])

    def push(slot):
        return pltpu.make_async_copy(held.at[slot], out.at[slot], out_sems.at[slot])

    named = []
    for o in range(OWNERS):
        row, col = o // 8, (o % 8) * CAP
        first = keys[row, col]
        last = -keys[4 + row, col]
        named += [(first < 1 << 20, first), ((first < 1 << 20) & (last != first), last)]

    def each(act):
        for slot, (wanted, key) in enumerate(named):
            pl.when(wanted)(functools.partial(act, slot, key))

    each(lambda slot, key: fetch(slot, jnp.minimum(key & 63, BLOCKS_DEV - 1)).start())
    for move in moves[2:]:
        move.wait()
    for h in range(OWNERS):
        seen[h] = 0
    row = me // 8
    col = (me % 8) * CAP
    for t in range(2 * CAP):
        block = rows_s[row, col + t] if t < CAP else cols_s[row, col + t - CAP]
        holder = holder_of(block)
        table[t] = 2 * holder + seen[holder]
        seen[holder] = 1
    live = count_s[me]
    for p in range(CAP):
        weight = jnp.where(rows_s[row, col + p] == cols_s[row, col + p], 1, 2)
        table[2 * CAP + p] = jnp.where(p < live, weight, 0)

    def forward(slot, key):
        fetch(slot, 0).wait()
        push(slot).start()

    each(forward)
    each(lambda slot, key: push(slot).wait())


def regroup_kernel(table, recv, gamma, out):
    for t in range(2 * CAP):
        block = recv[table[t]]
        dest = (t % CAP) // 2
        first = ((t % 2) + 2 * (t // CAP)) * GROUPS
        for g in range(GROUPS):
            out[dest, first + g] = block[:, g * LANES : (g + 1) * LANES]
    for p in range(CAP):
        weight = table[2 * CAP + p].astype(F32)
        out[p // 2, 4 * GROUPS + p % 2] = (gamma[p].astype(F32) * weight).astype(BF16)


def pair_kernel(recv, out, sent):
    def block(b):
        tiles = [recv[:, b * GROUPS + g].reshape(LANES, LANES) for g in range(GROUPS)]
        return jnp.concatenate(tiles, axis=1)

    left = []
    high = []
    low = []
    for q in range(2):
        stored = recv[:, 4 * GROUPS + q].reshape(LANES, LANES)
        half = jnp.dot(stored, block(2 + q), preferred_element_type=F32)
        top = half.astype(BF16)
        left.append(block(q))
        high.append(top)
        low.append((half - top.astype(F32)).astype(BF16))
    a = jnp.concatenate(left, axis=0)
    y = jnp.concatenate(high, axis=0)
    z = jnp.concatenate(low, axis=0)
    turned = jnp.concatenate([a.T, a.T, y.T, z.T], axis=1)
    other = jnp.concatenate([y, z, a, a], axis=0)
    out[0] = 0.25 * jnp.dot(turned[:WIDE], other[:, :WIDE], preferred_element_type=F32)
    right = jnp.dot(turned, other[:, WIDE:], preferred_element_type=F32)
    out[1] = 0.5 * right[:WIDE]
    out[2] = 0.25 * right[WIDE:]
    for k in range(3):
        sent[k] = out[k].astype(BF16)


def form_kernel(
    own, other, here, left_top, left_low, right_top, right_low, top_far, low_far, slope, out, far_top, far_low, sems
):
    first_half = pltpu.make_async_copy(top_far, far_top, sems.at[0])
    second_half = pltpu.make_async_copy(low_far, far_low, sems.at[1])
    first_half.start()
    second_half.start()
    chip = lax.axis_index("scn") // 2
    v = slope[...]
    one = v.astype(BF16)
    v = v - one.astype(F32)
    two = v.astype(BF16)
    v = v - two.astype(F32)
    fill = jnp.zeros((13, v.shape[1]), BF16)
    parts = jnp.concatenate([one, two, v.astype(BF16), fill], axis=0)
    first = (own[0] + other[0].astype(F32)).astype(BF16)
    cross = (own[1] + other[1].astype(F32)).astype(BF16)
    last = (own[2] + other[2].astype(F32)).astype(BF16)
    top = jnp.concatenate([first, parts[:, :WIDE]], axis=0)
    low = jnp.concatenate([cross, parts[:, WIDE:], last], axis=0)
    extra = WIDE + parts.shape[0]
    whole = (here.at[:WIDE, :], here.at[WIDE:, :])
    groups = ((0, whole), (1, (right_top, right_low)), (3, (left_top, left_low)), (2, (far_top, far_low)))
    for step, halves in groups:
        if step == 2:
            first_half.wait()
            second_half.wait()
        upper = halves[0][...]
        lower = halves[1][...]
        image = jnp.dot(low, lower, preferred_element_type=F32)
        more = image[:extra] + jnp.dot(top, upper, preferred_element_type=F32)
        total = jnp.sum(more[:WIDE] * upper.astype(F32) + image[extra:] * lower.astype(F32), axis=0, keepdims=True)
        out[(chip + step) & 3] = total + jnp.sum(more[WIDE:], axis=0, keepdims=True)


def ring(step):
    return [(i, (i + step) % PARTS) for i in range(PARTS)]


def body(loadings, draws, delta, gamma, pair_rows, pair_cols, pair_count):
    columns = draws.shape[1]
    depth = loadings.shape[1]
    upper, lower = draws[: depth // 2], draws[depth // 2 :]
    left_top = lax.ppermute(upper, "scn", ring(2))
    right_low = lax.ppermute(lower, "scn", ring(-2))
    left_low = lax.ppermute(lower, "scn", ring(2))
    right_top = lax.ppermute(upper, "scn", ring(-2))
    far_top = lax.ppermute(left_top, "scn", ring(2))
    far_low = lax.ppermute(right_low, "scn", ring(-2))
    outgoing, table = pl.pallas_call(
        pick_kernel,
        out_shape=(
            jax.ShapeDtypeStruct((2 * OWNERS, SLICE, depth), BF16),
            jax.ShapeDtypeStruct((3 * CAP,), jnp.int32),
        ),
        in_specs=[HBM, HBM, HBM, HBM],
        out_specs=(HBM, SMEM),
        scratch_shapes=[
            pltpu.VMEM((4, LANES), jnp.int32),
            pltpu.VMEM((4, LANES), jnp.int32),
            pltpu.SMEM((4, LANES), jnp.int32),
            pltpu.SMEM((4, LANES), jnp.int32),
            pltpu.SMEM((OWNERS,), jnp.int32),
            pltpu.SMEM((OWNERS,), jnp.int32),
            pltpu.VMEM((2 * OWNERS, SLICE, depth), BF16),
            pltpu.SemaphoreType.DMA((2 * OWNERS,)),
            pltpu.SemaphoreType.DMA((2 * OWNERS,)),
            pltpu.SemaphoreType.DMA((5,)),
        ],
        compiler_params=GRANT,
        name="pick",
    )(
        away(pair_rows.reshape(4, LANES)),
        away(pair_cols.reshape(4, LANES)),
        away(pair_count),
        away(loadings),
    )
    arrived = lax.all_to_all(outgoing, "fac", split_axis=0, concat_axis=0, tiled=True)
    chip = lax.axis_index("scn") // 2
    quarter = loadings.shape[0] // (PARTS // 2)
    some = lax.dynamic_slice_in_dim(loadings, chip * quarter, quarter)
    shares = lax.dynamic_slice_in_dim(delta, chip * quarter, quarter)
    slope = jnp.sum(shares[:, None] * some.astype(F32), axis=0)
    grouped = pl.pallas_call(
        regroup_kernel,
        out_shape=pltpu.VMEM((PARTS, 18, SLICE, LANES), BF16),
        in_specs=[SMEM, VMEM, VMEM],
        out_specs=VMEM,
        compiler_params=GRANT,
        name="regroup",
    )(table, near(arrived), gamma)
    pairs = lax.all_to_all(grouped, "scn", split_axis=0, concat_axis=0, tiled=True)
    own, sent = pl.pallas_call(
        pair_kernel,
        out_shape=(pltpu.VMEM((3, WIDE, WIDE), F32), pltpu.VMEM((3, WIDE, WIDE), BF16)),
        in_specs=[VMEM],
        out_specs=(VMEM, VMEM),
        compiler_params=GRANT,
        name="pair",
    )(near(pairs))
    other = lax.ppermute(sent, "scn", [(i, i ^ 1) for i in range(PARTS)])
    spread = pl.pallas_call(
        form_kernel,
        out_shape=pltpu.VMEM((PARTS // 2, 1, columns), F32),
        in_specs=[VMEM] * 7 + [HBM, HBM, VMEM],
        out_specs=VMEM,
        scratch_shapes=[
            pltpu.VMEM((depth // 2, columns), BF16),
            pltpu.VMEM((depth // 2, columns), BF16),
            pltpu.SemaphoreType.DMA((2,)),
        ],
        compiler_params=GRANT,
        name="form",
    )(near(own), near(other), draws, near(left_top), near(left_low), near(right_top), near(right_low), away(far_top), away(far_low), slope.reshape(1, depth))
    chips = [[c + 2 * x for x in range(PARTS // 2)] for c in range(2)]
    along = lax.all_to_all(
        spread, "scn", split_axis=0, concat_axis=0, tiled=True, axis_index_groups=chips
    )
    mine = jnp.broadcast_to(jnp.sum(along, axis=0)[None], (OWNERS, 1, columns))
    every = lax.all_to_all(mine, "fac", split_axis=0, concat_axis=0, tiled=True)
    return jnp.sum(every, axis=0).reshape(-1)


def solution(mesh):
    in_specs = (P("fac", None), P(None, "scn"), P("fac"), P("fac", "scn", None), P(), P(), P())
    out_specs = P("scn")
    return jax.shard_map(body, mesh=mesh, in_specs=in_specs, out_specs=out_specs, check_vma=False)
```

```python
import jax
import jax.numpy as jnp
from jax import lax
from jax.experimental import pallas as pl
from jax.experimental.pallas import tpu as pltpu
from jax.sharding import PartitionSpec as P


F32 = jnp.float32
BF16 = jnp.bfloat16
VMEM = pl.BlockSpec(memory_space=pltpu.VMEM)
SMEM = pl.BlockSpec(memory_space=pltpu.SMEM)
HBM = pl.BlockSpec(memory_space=pltpu.HBM)
GRANT = pltpu.CompilerParams(vmem_limit_bytes=24 * 1024 * 1024)
LANES = 128
OWNERS = 32
PARTS = 8
CAP = 16
BLOCKS_DEV = 48
SLICE = 16
GROUPS = 4
WIDE = 256


def near(x):
    return pltpu.with_memory_space_constraint(x, pltpu.VMEM)


def away(x):
    return pltpu.with_memory_space_constraint(x, pltpu.HBM)


def holder_of(block):
    return (block * 1366) >> 16


def pick_kernel(
    rows, cols, count, loadings, out, table,
    rows_v, cols_v, rows_s, cols_s, count_s, seen, sems, small,
):
    me = lax.axis_index("fac")
    part = lax.axis_index("scn")
    pairs = ((rows, rows_v), (cols, cols_v), (rows, rows_s), (cols, cols_s), (count, count_s))
    moves = [pltpu.make_async_copy(a, b, small.at[i]) for i, (a, b) in enumerate(pairs)]
    for move in moves:
        move.start()
    moves[0].wait()
    moves[1].wait()
    lane = lax.broadcasted_iota(jnp.int32, rows_v.shape, 1) & (CAP - 1)

    def keyed(blocks, first_slot):
        holder = holder_of(blocks)
        key = (lane + first_slot) * 64 + (blocks - holder * BLOCKS_DEV)
        mine = holder == me
        return jnp.where(mine, key, 1 << 20), jnp.where(mine, -key, 1)

    low_r, high_r = keyed(rows_v[...], 0)
    low_c, high_c = keyed(cols_v[...], CAP)
    keys = jnp.concatenate([jnp.minimum(low_r, low_c), jnp.minimum(high_r, high_c)], axis=0)
    for shift in (1, 2, 4, 8):
        keys = jnp.minimum(keys, pltpu.roll(keys, LANES - shift, 1))

    def fetch(slot, offset):
        start = pl.multiple_of(offset * LANES + part * SLICE, SLICE)
        return pltpu.make_async_copy(loadings.at[pl.ds(start, SLICE), :], out.at[slot], sems.at[slot])

    for o in range(OWNERS):
        row, col = o // 8, (o % 8) * CAP
        fetch(2 * o, jnp.minimum(keys[row, col] & 63, BLOCKS_DEV - 1)).start()
        fetch(2 * o + 1, jnp.minimum((-keys[4 + row, col]) & 63, BLOCKS_DEV - 1)).start()
    for move in moves[2:]:
        move.wait()
    for h in range(OWNERS):
        seen[h] = 0
    row = me // 8
    col = (me % 8) * CAP
    for t in range(2 * CAP):
        block = rows_s[row, col + t] if t < CAP else cols_s[row, col + t - CAP]
        holder = holder_of(block)
        table[t] = 2 * holder + seen[holder]
        seen[holder] = 1
    live = count_s[me]
    for p in range(CAP):
        weight = jnp.where(rows_s[row, col + p] == cols_s[row, col + p], 1, 2)
        table[2 * CAP + p] = jnp.where(p < live, weight, 0)
    for slot in range(2 * OWNERS):
        fetch(slot, 0).wait()


def regroup_kernel(table, recv, gamma, out):
    for t in range(2 * CAP):
        block = recv[table[t]]
        dest = (t % CAP) // 2
        first = ((t % 2) + 2 * (t // CAP)) * GROUPS
        for g in range(GROUPS):
            out[dest, first + g] = block[:, g * LANES : (g + 1) * LANES]
    for p in range(CAP):
        weight = table[2 * CAP + p].astype(F32)
        out[p // 2, 4 * GROUPS + p % 2] = (gamma[p].astype(F32) * weight).astype(BF16)


def pair_kernel(recv, out, sent):
    def block(b):
        tiles = [recv[:, b * GROUPS + g].reshape(LANES, LANES) for g in range(GROUPS)]
        return jnp.concatenate(tiles, axis=1)

    left = []
    high = []
    low = []
    for q in range(2):
        stored = recv[:, 4 * GROUPS + q].reshape(LANES, LANES)
        half = jnp.dot(stored, block(2 + q), preferred_element_type=F32)
        top = half.astype(BF16)
        left.append(block(q))
        high.append(top)
        low.append((half - top.astype(F32)).astype(BF16))
    a = jnp.concatenate(left, axis=0)
    y = jnp.concatenate(high, axis=0)
    z = jnp.concatenate(low, axis=0)
    turned = jnp.concatenate([a.T, a.T, y.T, z.T], axis=1)
    other = jnp.concatenate([y, z, a, a], axis=0)
    out[0] = 0.25 * jnp.dot(turned[:WIDE], other[:, :WIDE], preferred_element_type=F32)
    right = jnp.dot(turned, other[:, WIDE:], preferred_element_type=F32)
    out[1] = 0.5 * right[:WIDE]
    out[2] = 0.25 * right[WIDE:]
    for k in range(3):
        sent[k] = out[k].astype(BF16)


def form_kernel(
    own, other, here, left_top, left_low, right_top, right_low, top_far, low_far, slope,
    mine, across, sent, out, far_top, far_low, sems,
):
    first_half = pltpu.make_async_copy(top_far, far_top, sems.at[0])
    second_half = pltpu.make_async_copy(low_far, far_low, sems.at[1])
    first_half.start()
    second_half.start()
    chip = lax.axis_index("scn") // 2
    v = slope[...]
    one = v.astype(BF16)
    v = v - one.astype(F32)
    two = v.astype(BF16)
    v = v - two.astype(F32)
    fill = jnp.zeros((13, v.shape[1]), BF16)
    parts = jnp.concatenate([one, two, v.astype(BF16), fill], axis=0)
    first = (own[0] + other[0].astype(F32)).astype(BF16)
    cross = (own[1] + other[1].astype(F32)).astype(BF16)
    last = (own[2] + other[2].astype(F32)).astype(BF16)
    top = jnp.concatenate([first, parts[:, :WIDE]], axis=0)
    low = jnp.concatenate([cross, parts[:, WIDE:], last], axis=0)
    extra = WIDE + parts.shape[0]
    whole = (here.at[:WIDE, :], here.at[WIDE:, :])
    groups = ((0, whole), (1, (right_top, right_low)), (3, (left_top, left_low)), (2, (far_top, far_low)))
    for step, halves in groups:
        if step == 2:
            first_half.wait()
            second_half.wait()
        upper = halves[0][...]
        lower = halves[1][...]
        image = jnp.dot(low, lower, preferred_element_type=F32)
        more = image[:extra] + jnp.dot(top, upper, preferred_element_type=F32)
        total = jnp.sum(more[:WIDE] * upper.astype(F32) + image[extra:] * lower.astype(F32), axis=0, keepdims=True)
        group = (chip + step) & 3
        beside = group == (chip ^ 1)
        place = jnp.where(beside, 1, jnp.where(group == 3 - chip, 2, 3)) if step else 0
        out[place] = total + jnp.sum(more[WIDE:], axis=0, keepdims=True)
    mine[...] = out[0]
    across[...] = out[1]
    sent[0] = out[2]
    sent[1] = out[3]


def ring(step):
    return [(i, (i + step) % PARTS) for i in range(PARTS)]


def body(loadings, draws, delta, gamma, pair_rows, pair_cols, pair_count):
    columns = draws.shape[1]
    depth = loadings.shape[1]
    upper, lower = draws[: depth // 2], draws[depth // 2 :]
    left_top = lax.ppermute(upper, "scn", ring(2))
    right_low = lax.ppermute(lower, "scn", ring(-2))
    left_low = lax.ppermute(lower, "scn", ring(2))
    right_top = lax.ppermute(upper, "scn", ring(-2))
    far_top = lax.ppermute(left_top, "scn", ring(2))
    far_low = lax.ppermute(right_low, "scn", ring(-2))
    outgoing, table = pl.pallas_call(
        pick_kernel,
        out_shape=(
            pltpu.VMEM((2 * OWNERS, SLICE, depth), BF16),
            jax.ShapeDtypeStruct((3 * CAP,), jnp.int32),
        ),
        in_specs=[HBM, HBM, HBM, HBM],
        out_specs=(VMEM, SMEM),
        scratch_shapes=[
            pltpu.VMEM((4, LANES), jnp.int32),
            pltpu.VMEM((4, LANES), jnp.int32),
            pltpu.SMEM((4, LANES), jnp.int32),
            pltpu.SMEM((4, LANES), jnp.int32),
            pltpu.SMEM((OWNERS,), jnp.int32),
            pltpu.SMEM((OWNERS,), jnp.int32),
            pltpu.SemaphoreType.DMA((2 * OWNERS,)),
            pltpu.SemaphoreType.DMA((5,)),
        ],
        compiler_params=GRANT,
        name="pick",
    )(
        away(pair_rows.reshape(4, LANES)),
        away(pair_cols.reshape(4, LANES)),
        away(pair_count),
        away(loadings),
    )
    arrived = lax.all_to_all(outgoing, "fac", split_axis=0, concat_axis=0, tiled=True)
    chip = lax.axis_index("scn") // 2
    quarter = loadings.shape[0] // (PARTS // 2)
    some = lax.dynamic_slice_in_dim(loadings, chip * quarter, quarter)
    shares = lax.dynamic_slice_in_dim(delta, chip * quarter, quarter)
    slope = jnp.sum(shares[:, None] * some.astype(F32), axis=0)
    grouped = pl.pallas_call(
        regroup_kernel,
        out_shape=pltpu.VMEM((PARTS, 18, SLICE, LANES), BF16),
        in_specs=[SMEM, VMEM, VMEM],
        out_specs=VMEM,
        compiler_params=GRANT,
        name="regroup",
    )(table, near(arrived), gamma)
    pairs = lax.all_to_all(grouped, "scn", split_axis=0, concat_axis=0, tiled=True)
    own, sent = pl.pallas_call(
        pair_kernel,
        out_shape=(pltpu.VMEM((3, WIDE, WIDE), F32), pltpu.VMEM((3, WIDE, WIDE), BF16)),
        in_specs=[VMEM],
        out_specs=(VMEM, VMEM),
        compiler_params=GRANT,
        name="pair",
    )(near(pairs))
    other = lax.ppermute(sent, "scn", [(i, i ^ 1) for i in range(PARTS)])
    mine, across, send = pl.pallas_call(
        form_kernel,
        out_shape=(
            pltpu.VMEM((1, columns), F32),
            pltpu.VMEM((1, columns), F32),
            pltpu.VMEM((2, 1, columns), F32),
        ),
        in_specs=[VMEM] * 7 + [HBM, HBM, VMEM],
        out_specs=(VMEM, VMEM, VMEM),
        scratch_shapes=[
            pltpu.VMEM((4, 1, columns), F32),
            pltpu.VMEM((depth // 2, columns), BF16),
            pltpu.VMEM((depth // 2, columns), BF16),
            pltpu.SemaphoreType.DMA((2,)),
        ],
        compiler_params=GRANT,
        name="form",
    )(near(own), near(other), draws, near(left_top), near(left_low), near(right_top), near(right_low), away(far_top), away(far_low), slope.reshape(1, depth))
    near_sum = lax.ppermute(send, "scn", [(i, 6 - i + 2 * (i % 2)) for i in range(PARTS)])
    across = across + near_sum[1]
    over = lax.ppermute(across, "scn", [(i, i ^ 2) for i in range(PARTS)])
    total = mine + near_sum[0] + over
    spread = jnp.broadcast_to(total[None], (OWNERS, 1, columns))
    every = lax.all_to_all(spread, "fac", split_axis=0, concat_axis=0, tiled=True)
    return jnp.sum(every, axis=0).reshape(-1)


def solution(mesh):
    in_specs = (P("fac", None), P(None, "scn"), P("fac"), P("fac", "scn", None), P(), P(), P())
    out_specs = P("scn")
    return jax.shard_map(body, mesh=mesh, in_specs=in_specs, out_specs=out_specs, check_vma=False)
```
